256 devices in a mesh: dp: 8 (over z), expert: 32 (over x, y, core).
Axes of the slice: x: 4, y: 4, z: 8, core: 2. Of those that a mesh axis runs over, the one named last changes fastest.
Arguments:
- tokens: bfloat16 [32768, 2048], P(('dp', 'expert')), may hold values from -24 to 24
- expert_ids: int32 [32768, 2], P(('dp', 'expert')), may hold values from 0 to 31, all different within a row; in each aligned block of 128 rows (0 to 127, 128 to 255, ...) at most 16 rows name the same one
- gate_probs: float32 [32768, 2], P(('dp', 'expert')), may hold values from 0.1 to 1
- w_gate: bfloat16 [32, 2048, 768], P('expert'), may hold values from -0.125 to 0.125
- w_up: bfloat16 [32, 2048, 768], P('expert'), may hold values from -0.125 to 0.125
- w_down: bfloat16 [32, 2048, 768], P('expert'), may hold values from -0.21875 to 0.21875
- out_grad: bfloat16 [32768, 2048], P(('dp', 'expert')), may hold values from -6 to 6
Outputs:
- mixed: bfloat16 [32768, 2048], P(('dp', 'expert'))
- tokens_grad: bfloat16 [32768, 2048], P(('dp', 'expert'))
- grad_gate: bfloat16 [32, 2048, 768], P('expert', 'dp')
- grad_up: bfloat16 [32, 2048, 768], P('expert', 'dp')
- grad_down: bfloat16 [32, 2048, 768], P('expert', 'dp')
The draws below stay inside these ranges and needn't reach their ends.
Inputs may be any that keep to these rules, and one draw needn't show every extreme that they name: `expert_ids`: within each group of 128 tokens no expert is chosen by more than 16 tokens, and some expert reaches 16; a token's 2 experts differ; every expert is chosen somewhere.
All inputs are finite; a program needn't handle non-finite values.
Results may differ from the reference program's by a relative error of at most 0.014.
Values may be sent and summed in bfloat16 or wider, within the bound.
A program may use at most 128 MiB of HBM per device.

```python
import math
import jax
import jax.numpy as jnp
import numpy as np
from jax import lax

D = 2048
H = 768
TOP = 2
TOK_DEV = 128
EXPERTS = 32
CAP = 16
TOKENS = 32768
N_DP = 8
N_EXPERT = 32


def raised(entries, own_key, source, target, parts, factor):
    def block_of(dim):
        return (jnp.arange(entries.shape[dim]) // (entries.shape[dim] // parts)).reshape((-1,) + (1,) * (entries.ndim - 1 - dim))

    one_side = jax.random.permutation(own_key, parts)[block_of(target)]
    other_side = (block_of(target) + parts // 2) % parts
    return jnp.where((block_of(source) == one_side) | (block_of(source) == other_side), factor * entries, entries)


def levels(stream_key, shape, split, smallest, top_value):
    factor_of, own = 1.0, jax.random.fold_in(stream_key, 6)
    for dim, blocks in split:
        steps = jnp.exp(jax.random.uniform(jax.random.fold_in(own, dim), (blocks,), jnp.float32, smallest / len(split), top_value / len(split)))
        factor_of = factor_of * jnp.repeat(steps, shape[dim] // blocks).reshape([-1 if axis == dim else 1 for axis in range(len(shape))])
    return factor_of


def routed_block(rng, own, number, rows, amount, top, limit, skew):
    ranking = jax.random.permutation(rng, amount)
    crowded, usual = portions_of(amount, rows * top, limit, skew, True), portions_of(amount, rows * top, limit, skew, False)
    places = jnp.arange(amount)

    def named(tallies, offset_by):
        used = int((tallies > 0).sum())
        fixed = max(1, used // 4)
        shifted = fixed + (places - fixed + offset_by * (used - fixed)) % max(1, amount - fixed)
        return jnp.zeros((amount,), jnp.int32).at[ranking[jnp.where(places < fixed, places, shifted)]].set(jnp.asarray(tallies, jnp.int32))

    tallies = jnp.where(number % 4 == 0, named(crowded, number // 4), named(usual, number - number // 4 - 1))
    mixed = jax.random.permutation(jax.random.fold_in(own, 3), amount)
    source_of, sink = mixed[0:amount // 2 * 2:2], mixed[1:amount // 2 * 2:2]
    slack = jnp.minimum(tallies[source_of] - 1, limit - tallies[sink]) // 2
    slack = jnp.where((source_of == ranking[0]) | (sink == ranking[0]) | (tallies[sink] == 0), 0, jnp.maximum(slack, 0))
    shifted = jax.random.randint(jax.random.fold_in(own, 4), (amount // 2,), 0, 1 << 20) % (slack + 1)
    tallies = tallies.at[source_of].add(-shifted).at[sink].add(shifted)
    labels = jnp.searchsorted(jnp.cumsum(tallies), jnp.arange(rows * top), side="right").astype(jnp.int32)
    table = labels.reshape(top, rows).T
    table = table[jax.random.permutation(jax.random.fold_in(own, 1), rows)]
    offset_by = jax.random.randint(jax.random.fold_in(own, 2), (rows, 1), 0, top)
    return jnp.take_along_axis(table, (jnp.arange(top)[None, :] + offset_by) % top, axis=1)


def portions_of(count, total, reach, slope, full):
    portions = [(1 << 20) // math.isqrt(grade ** slope) + 1 for grade in range(1, count + 1)]
    largest = reach if full else min(reach, max(-(-total // count), total * portions[0] // sum(portions)))
    least = 1 if total - largest >= count - 1 else 0
    holding, spare = [largest] + [least] * (count - 1), total - largest - least * (count - 1)
    while spare > 0:
        free = [i for i in range(1, count) if holding[i] < largest] or [i for i in range(1, count) if holding[i] < reach]
        pool, budget = sum([portions[i] for i in free]), spare
        for i in free:
            addition = min(reach - holding[i], max(1, budget * portions[i] // pool), spare)
            holding[i] = holding[i] + addition
            spare = spare - addition
    return np.array(holding)


def normal_values(own_key, shape, spread, limit, cuts=(), held_as=jnp.bfloat16):
    array = spread * jax.random.normal(own_key, shape, jnp.float32)
    if cuts:
        array = array * levels(own_key, shape, cuts, -0.22, 0.18)
    return jnp.clip(array, -limit, limit).astype(held_as)


def gaussian_with(rng, extent, deviation, most, cuts, heavy, held_as=jnp.bfloat16):
    result = deviation * jax.random.normal(rng, extent, jnp.float32)
    if cuts:
        result = result * levels(rng, extent, cuts, -0.22, 0.18)
    return jnp.clip(raised(result, jax.random.fold_in(rng, 3), *heavy), -most, most).astype(held_as)


def setup_inputs(seed: int = 0) -> dict:
    key_of = jax.random.split(jax.random.key(seed), 8)
    tokens = gaussian_with(key_of[0], (TOKENS, D), 1.0, 24.0, ((0, 256),), (0, 1, 256, 6.0))
    expert_ids_keys = jax.random.split(jax.random.fold_in(key_of[1], 1), TOKENS // TOK_DEV)
    expert_ids_turns = jax.random.permutation(jax.random.fold_in(key_of[1], 3), TOKENS // TOK_DEV)
    expert_ids = jax.vmap(lambda own, number: routed_block(jax.random.fold_in(key_of[1], 2), own, number, TOK_DEV, EXPERTS, TOP, CAP, 2))(expert_ids_keys, expert_ids_turns).reshape((TOKENS, TOP))
    gate_probs = jnp.clip(0.1 + 0.9 * jax.random.uniform(key_of[2], (TOKENS, TOP), jnp.float32) ** levels(key_of[2], (TOKENS, TOP), ((0, 256),), -0.2, 0.2), 0.1, 1.0)
    w_gate = normal_values(key_of[3], (EXPERTS, D, H), D ** -0.5, 0.125, ((0, 32),))
    w_up = normal_values(key_of[4], (EXPERTS, D, H), D ** -0.5, 0.125, ((0, 32),))
    w_down = normal_values(key_of[5], (EXPERTS, D, H), H ** -0.5, 0.21875, ((0, 32),))
    out_grad = normal_values(key_of[6], (TOKENS, D), 1.0, 6.0, ((0, 256),))
    return {"tokens": tokens, "expert_ids": expert_ids, "gate_probs": gate_probs, "w_gate": w_gate, "w_up": w_up, "w_down": w_down, "out_grad": out_grad}


def route_slots(ids):
    flat = ids.reshape(-1).astype(jnp.int32)
    onehot = (flat[:, None] == jnp.arange(EXPERTS, dtype=jnp.int32)[None, :]).astype(jnp.int32)
    before = jnp.cumsum(onehot, axis=0) - onehot
    position = jnp.sum(before * onehot, axis=1).astype(jnp.int32)
    return (flat * CAP + position).astype(jnp.int32)


def place_rows(rows, slot):
    empty = jnp.zeros((EXPERTS * CAP, D), rows.dtype)
    return empty.at[slot].set(rows)


def pick_rows(table, slot):
    return jnp.take(table, slot, axis=0)


def reference(tokens, expert_ids, gate_probs, w_gate, w_up, w_down, out_grad):
    wg32 = w_gate.astype(jnp.float32)
    wu32 = w_up.astype(jnp.float32)
    wd32 = w_down.astype(jnp.float32)
    tok_sets = tokens.reshape(N_DP, N_EXPERT, TOK_DEV, D)
    id_sets = expert_ids.reshape(N_DP, N_EXPERT, TOK_DEV, TOP)
    prob_sets = gate_probs.reshape(N_DP, N_EXPERT, TOK_DEV, TOP)
    dy_sets = out_grad.reshape(N_DP, N_EXPERT, TOK_DEV, D)

    def one_set(carry, inputs):
        xs, ids, probs, dys = inputs
        slots = jax.vmap(route_slots)(ids)
        x_routes = jnp.repeat(xs, TOP, axis=1)
        x_slot = jax.vmap(place_rows)(x_routes, slots).reshape(N_EXPERT, EXPERTS, CAP, D)
        xf = x_slot.astype(jnp.float32)
        gact = jnp.einsum('secd,edh->sech', xf, wg32)
        uact = jnp.einsum('secd,edh->sech', xf, wu32)
        hidden = (jax.nn.silu(gact) * uact).astype(jnp.bfloat16)
        o_slot = jnp.einsum('sech,edh->secd', hidden.astype(jnp.float32), wd32).astype(jnp.bfloat16)
        picked = jax.vmap(pick_rows)(o_slot.reshape(N_EXPERT, EXPERTS * CAP, D), slots)
        picked = picked.astype(jnp.float32).reshape(N_EXPERT, TOK_DEV, TOP, D)
        mixed = jnp.sum(picked * probs[..., None], axis=2).astype(jnp.bfloat16)
        dy_routes = jnp.repeat(dys, TOP, axis=1).astype(jnp.float32) * probs.reshape(N_EXPERT, TOK_DEV * TOP)[..., None]
        dy_slot = jax.vmap(place_rows)(dy_routes.astype(jnp.bfloat16), slots).reshape(N_EXPERT, EXPERTS, CAP, D)
        dyf = dy_slot.astype(jnp.float32)
        dh = jnp.einsum('secd,edh->sech', dyf, wd32)
        sig = jax.nn.sigmoid(gact)
        dg = (dh * uact * sig * (1.0 + gact * (1.0 - sig))).astype(jnp.bfloat16)
        du = (dh * gact * sig).astype(jnp.bfloat16)
        dgf = dg.astype(jnp.float32)
        duf = du.astype(jnp.float32)
        dx_slot = (jnp.einsum('sech,edh->secd', dgf, wg32) + jnp.einsum('sech,edh->secd', duf, wu32)).astype(jnp.bfloat16)
        dx_picked = jax.vmap(pick_rows)(dx_slot.reshape(N_EXPERT, EXPERTS * CAP, D), slots)
        dx_tok = jnp.sum(dx_picked.astype(jnp.float32).reshape(N_EXPERT, TOK_DEV, TOP, D), axis=2).astype(jnp.bfloat16)
        part_g = jnp.einsum('secd,sech->edh', xf, dgf).astype(jnp.bfloat16)
        part_u = jnp.einsum('secd,sech->edh', xf, duf).astype(jnp.bfloat16)
        part_d = jnp.einsum('secd,sech->edh', dyf, hidden.astype(jnp.float32)).astype(jnp.bfloat16)
        part_g, part_u, part_d = lax.optimization_barrier((part_g, part_u, part_d))
        carry = (carry[0] + part_g.astype(jnp.float32), carry[1] + part_u.astype(jnp.float32), carry[2] + part_d.astype(jnp.float32))
        return carry, (mixed, dx_tok)

    zero = jnp.zeros((EXPERTS, D, H), jnp.float32)
    sums, outs = lax.scan(one_set, (zero, zero, zero), (tok_sets, id_sets, prob_sets, dy_sets))
    mixed = outs[0].reshape(TOKENS, D)
    tokens_grad = outs[1].reshape(TOKENS, D)
    return (mixed, tokens_grad, sums[0].astype(jnp.bfloat16), sums[1].astype(jnp.bfloat16), sums[2].astype(jnp.bfloat16))
```

```python
import functools

import jax
import jax.numpy as jnp
from jax import lax
from jax.experimental import pallas as pl
from jax.experimental.pallas import tpu as pltpu
from jax.sharding import PartitionSpec as P

MESH = pl.DeviceIdType.MESH
F32 = jnp.float32
BF16 = jnp.bfloat16

NX, NY, NC = 4, 4, 2
CHIPS = NX * NY
PEERS = CHIPS * NC
NZ = 8
TOK = 128
TOP = 2
CAP = 16
SLOTS = PEERS * CAP
D = 2048
H = 768
SHARD = D // NZ
HALF = SHARD // 2
PIECES = 7


def dot(a, b):
    return jnp.dot(a, b, preferred_element_type=F32)


def dot_rhs_t(a, b):
    return lax.dot_general(a, b, (((1,), (1,)), ((), ())), preferred_element_type=F32)


def place(index):
    return index // (NY * NC), lax.rem(index // NC, NY), lax.rem(index, NC)


def offset(j):
    p = lax.rem(j * 7, CHIPS)
    return p // NY, lax.rem(p, NY)


def ahead(x, y, core, j):
    dx, dy = offset(j)
    return (lax.rem(x + dx, NX) * NY + lax.rem(y + dy, NY)) * NC + core


def behind(x, y, core, j):
    dx, dy = offset(j)
    return (lax.rem(x + NX - dx, NX) * NY + lax.rem(y + NY - dy, NY)) * NC + core


def rows_of(block):
    return pl.ds(pl.multiple_of(block * CAP, CAP), CAP)


def loop(low, high, body):
    def step(i, carry):
        body(i)
        return carry

    lax.fori_loop(low, high, step, 0)


def kernel(
    ids_ref, prob_ref, tok_hbm, og_hbm, wg_hbm, wu_hbm, wd_hbm,
    mixed_ref, tgrad_ref, gg_ref, gu_ref, gd_ref,
    tok, og, wg, wu, wd,
    xs, ds, xr, dr, hid, dg, du, ca, cb,
    ov, dxv, orv, dxr,
    sp, sq, rp, rq, acc,
    load_sem, xss, dss, oss, dxss, xrs, drs, ors, dxrs, pss, qss, prs, qrs,
):
    me = lax.axis_index("expert")
    z = lax.axis_index("dp")
    x, y, core = place(me)
    up = lax.rem(z + 1, NZ)
    down = lax.rem(z + NZ - 1, NZ)

    loads = [
        pltpu.make_async_copy(src, dst, load_sem.at[i])
        for i, (src, dst) in enumerate(
            [(tok_hbm, tok), (og_hbm, og), (wg_hbm.at[0], wg), (wu_hbm.at[0], wu), (wd_hbm.at[0], wd)]
        )
    ]
    for load in loads:
        load.start()

    barrier = pltpu.get_barrier_semaphore()

    def greet(i):
        pl.semaphore_signal(
            barrier, inc=1, device_id={"expert": lax.rem(me + i, PEERS)}, device_id_type=MESH
        )

    loop(1, PEERS, greet)
    for other in (up, down):
        pl.semaphore_signal(barrier, inc=1, device_id={"dp": other}, device_id_type=MESH)

    sub = lax.broadcasted_iota(jnp.int32, (TOK, TOK), 0)
    lane = lax.broadcasted_iota(jnp.int32, (TOK, TOK), 1)
    eye = sub == lane
    lane_f = lane.astype(F32)

    def to_col(row):
        return jnp.sum(jnp.where(eye, row, 0.0), axis=1, keepdims=True)

    def to_row(col):
        return jnp.sum(jnp.where(eye, col, 0.0), axis=0, keepdims=True)

    ids_f = ids_ref[...].astype(F32)
    probs = prob_ref[...]
    id_col = [to_col(ids_f[k : k + 1]) for k in range(TOP)]
    hot = [lane_f == id_col[k] for k in range(TOP)]
    chosen = jnp.where(hot[0] | hot[1], 1.0, 0.0).astype(BF16)
    earlier = jnp.where(lane < sub, 1.0, 0.0).astype(BF16)
    before = dot(earlier, chosen)
    slot_col = [
        id_col[k] * CAP + jnp.sum(jnp.where(hot[k], before, 0.0), axis=1, keepdims=True)
        for k in range(TOP)
    ]
    slot_row = [to_row(slot_col[k]) for k in range(TOP)]
    prob_row = [probs[k : k + 1] for k in range(TOP)]
    prob_col = [to_col(prob_row[k]) for k in range(TOP)]
    slot_of = lax.broadcasted_iota(jnp.int32, (SLOTS, TOK), 0).astype(F32)
    owner = [slot_of == slot_row[k] for k in range(TOP)]
    pick = jnp.where(owner[0] | owner[1], 1.0, 0.0).astype(BF16)
    slot_prob = jnp.sum(
        jnp.where(owner[0], prob_row[0], 0.0) + jnp.where(owner[1], prob_row[1], 0.0),
        axis=1,
        keepdims=True,
    )

    WIDE = 512

    def wide(n):
        return pl.ds(pl.multiple_of(n * WIDE, WIDE), WIDE)

    loads[0].wait()

    def build_x(n):
        xs[:, wide(n)] = dot(pick, tok[:, wide(n)]).astype(BF16)

    loop(0, D // WIDE, build_x)
    pl.semaphore_wait(barrier, PEERS - 1 + 2)

    def to_expert(src, dst, send_sem, recv_sem, j, t):
        peer = ahead(x, y, t, j)
        return pltpu.make_async_remote_copy(
            src.at[rows_of(peer)],
            dst.at[rows_of(j * NC + core)],
            send_sem.at[t * CHIPS + j],
            recv_sem.at[j * NC + core],
            device_id={"expert": peer},
            device_id_type=MESH,
        )

    def own_block(src, dst, recv_sem):
        return pltpu.make_async_copy(src.at[rows_of(me)], dst.at[rows_of(core)], recv_sem.at[core])

    def dispatch(src, dst, send_sem, recv_sem, t):
        @pl.when(core == t)
        def _():
            own_block(src, dst, recv_sem).start()

        @pl.when(core != t)
        def _():
            to_expert(src, dst, send_sem, recv_sem, 0, t).start()

        loop(1, CHIPS, lambda j: to_expert(src, dst, send_sem, recv_sem, j, t).start())

    dispatch(xs, xr, xss, xrs, 0)
    loads[1].wait()

    def build_dy(n):
        ds[:, wide(n)] = (dot(pick, og[:, wide(n)]) * slot_prob).astype(BF16)

    loop(0, D // WIDE, build_dy)
    dispatch(ds, dr, dss, drs, 0)
    dispatch(xs, xr, xss, xrs, 1)
    dispatch(ds, dr, dss, drs, 1)

    def arrived(dst, recv_sem, i):
        pltpu.make_async_copy(dst.at[rows_of(i)], dst.at[rows_of(i)], recv_sem.at[i]).wait()

    TILE = 256
    MX = 256

    def tile(n):
        return pl.ds(pl.multiple_of(n * TILE, TILE), TILE)

    loads[2].wait()
    loads[3].wait()

    def forward(m):
        loop(0, MX // CAP, lambda i: arrived(xr, xrs, m * (MX // CAP) + i))
        rows = pl.ds(pl.multiple_of(m * MX, MX), MX)

        def columns(n):
            g = dot(xr[rows, :], wg[:, tile(n)])
            u = dot(xr[rows, :], wu[:, tile(n)])
            s = 1.0 / (1.0 + jnp.exp(-g))
            gs = g * s
            hid[rows, tile(n)] = (gs * u).astype(BF16)
            cb[rows, tile(n)] = gs
            ca[rows, tile(n)] = u * s * (1.0 + g * (1.0 - s))

        loop(0, H // TILE, columns)

    loop(0, SLOTS // MX, forward)

    loads[4].wait()
    MD = 128

    def backward(m):
        loop(0, MD // CAP, lambda i: arrived(dr, drs, m * (MD // CAP) + i))
        rows = pl.ds(pl.multiple_of(m * MD, MD), MD)

        def columns(n):
            dh = dot(dr[rows, :], wd[:, tile(n)])
            dg[rows, tile(n)] = (dh * ca[rows, tile(n)]).astype(BF16)
            du[rows, tile(n)] = (dh * cb[rows, tile(n)]).astype(BF16)

        loop(0, H // TILE, columns)

    loop(0, SLOTS // MD, backward)

    def own_part(shard, half, out):
        cols = pl.ds(pl.multiple_of(shard * SHARD + half * HALF, HALF), HALF)
        xt = jnp.transpose(xr[:, cols])
        out[0:HALF] = dot(xt, dg[...])
        out[HALF : 2 * HALF] = dot(xt, du[...])
        dt = jnp.transpose(dr[:, cols])
        out[2 * HALF : 3 * HALF] = dot(dt, hid[...])

    def shard_up(k):
        return lax.rem(z + 4 - (k + 1) // 2 + NZ, NZ), lax.rem(k + 1, 2)

    def shard_down(k):
        return lax.rem(z - 4 + (k + 1) // 2 + NZ, NZ), lax.rem(k, 2)

    def pass_on(src, dst, send_sem, recv_sem, k, to):
        return pltpu.make_async_remote_copy(
            src, dst.at[k], send_sem.at[k], recv_sem.at[k], device_id={"dp": to}, device_id_type=MESH
        )

    ways = (
        (shard_up, sp, rp, pss, prs, up),
        (shard_down, sq, rq, qss, qrs, down),
    )

    def first(k):
        for which, staged, got, send_sem, recv_sem, to in ways:
            shard, half = which(k)
            own_part(shard, half, acc)
            staged[k] = acc[...].astype(BF16)
            pass_on(staged.at[k], got, send_sem, recv_sem, k, to).start()

    loop(0, 2, first)

    def to_token(src, dst, send_sem, recv_sem, i):
        j, c = i // NC, lax.rem(i, NC)
        peer = behind(x, y, c, j)
        return pltpu.make_async_remote_copy(
            src.at[rows_of(i)],
            dst.at[rows_of(me)],
            send_sem.at[i],
            recv_sem.at[me],
            device_id={"expert": peer},
            device_id_type=MESH,
        )

    def give_back(src, dst, send_sem, recv_sem, i):
        @pl.when(i == core)
        def _():
            pltpu.make_async_copy(src.at[rows_of(i)], dst.at[rows_of(me)], recv_sem.at[me]).start()

        @pl.when(i != core)
        def _():
            to_token(src, dst, send_sem, recv_sem, i).start()

    def outputs(m):
        rows = pl.ds(pl.multiple_of(m * MD, MD), MD)

        def columns(n):
            ov[rows, tile(n)] = dot_rhs_t(hid[rows, :], wd[tile(n), :]).astype(BF16)
            dxv[rows, tile(n)] = (
                dot_rhs_t(dg[rows, :], wg[tile(n), :]) + dot_rhs_t(du[rows, :], wu[tile(n), :])
            ).astype(BF16)

        loop(0, D // TILE, columns)

        def send(i):
            give_back(ov, orv, oss, ors, m * (MD // CAP) + i)
            give_back(dxv, dxr, dxss, dxrs, m * (MD // CAP) + i)

        loop(0, MD // CAP, send)

    def later(k):
        for which, staged, got, send_sem, recv_sem, to in ways:
            shard, half = which(k)
            own_part(shard, half, acc)
            pass_on(got.at[k - 2], got, send_sem, recv_sem, k - 2, to).wait_recv()
            got[k - 2] = (acc[...] + got[k - 2].astype(F32)).astype(BF16)
            pass_on(got.at[k - 2], got, send_sem, recv_sem, k, to).start()

    def outputs_and_later(k):
        outputs(k - 2)
        later(k)

    loop(2, 2 + SLOTS // MD, outputs_and_later)
    loop(2 + SLOTS // MD, PIECES, later)

    loop(0, PEERS, lambda i: arrived(orv, ors, i))
    loop(0, PEERS, lambda i: arrived(dxr, dxrs, i))
    slot_lane = lax.broadcasted_iota(jnp.int32, (TOK, SLOTS), 1).astype(F32)
    route = [slot_lane == slot_col[k] for k in range(TOP)]
    one = [jnp.where(route[k], 1.0, 0.0).astype(BF16) for k in range(TOP)]
    either = jnp.where(route[0] | route[1], 1.0, 0.0).astype(BF16)

    def combine(n):
        mixed_ref[:, wide(n)] = (
            dot(one[0], orv[:, wide(n)]) * prob_col[0] + dot(one[1], orv[:, wide(n)]) * prob_col[1]
        ).astype(BF16)
        tgrad_ref[:, wide(n)] = dot(either, dxr[:, wide(n)]).astype(BF16)

    loop(0, D // WIDE, combine)

    for half, (k_up, k_down) in enumerate(((5, 6), (6, 5))):
        own_part(z, half, acc)
        pass_on(rp.at[k_up], rp, pss, prs, k_up, up).wait_recv()
        pass_on(rq.at[k_down], rq, qss, qrs, k_down, down).wait_recv()
        for w, out in enumerate((gg_ref, gu_ref, gd_ref)):
            rows = pl.ds(w * HALF, HALF)
            out[0, half * HALF : (half + 1) * HALF] = (
                acc[rows] + rp[k_up, rows].astype(F32) + rq[k_down, rows].astype(F32)
            ).astype(BF16)

    def sent(src, dst, send_sem, recv_sem, i):
        to_expert(src, dst, send_sem, recv_sem, lax.rem(i, CHIPS), i // CHIPS).wait_send()

    def all_sent(i):
        @pl.when(i != core * CHIPS)
        def _():
            sent(xs, xr, xss, xrs, i)
            sent(ds, dr, dss, drs, i)

        @pl.when(i != core)
        def _():
            to_token(ov, orv, oss, ors, i).wait_send()
            to_token(dxv, dxr, dxss, dxrs, i).wait_send()

    loop(0, PEERS, all_sent)

    def passed(k):
        pass_on(rp.at[k], rp, pss, prs, k, up).wait_send()
        pass_on(rq.at[k], rq, qss, qrs, k, down).wait_send()

    loop(0, PIECES, passed)


def local(tokens, expert_ids, gate_probs, w_gate, w_up, w_down, out_grad):
    vmem = pl.BlockSpec(memory_space=pltpu.VMEM)
    hbm = pl.BlockSpec(memory_space=pl.ANY)
    dma = pltpu.SemaphoreType.DMA
    slots = lambda: pltpu.VMEM((SLOTS, D), BF16)
    acts = lambda dtype: pltpu.VMEM((SLOTS, H), dtype)
    return pl.pallas_call(
        kernel,
        out_shape=(
            jax.ShapeDtypeStruct((TOK, D), BF16),
            jax.ShapeDtypeStruct((TOK, D), BF16),
            jax.ShapeDtypeStruct((1, SHARD, H), BF16),
            jax.ShapeDtypeStruct((1, SHARD, H), BF16),
            jax.ShapeDtypeStruct((1, SHARD, H), BF16),
        ),
        in_specs=[vmem, vmem] + [hbm] * 5,
        out_specs=(vmem,) * 5,
        scratch_shapes=[
            pltpu.VMEM((TOK, D), BF16),
            pltpu.VMEM((TOK, D), BF16),
            pltpu.VMEM((D, H), BF16),
            pltpu.VMEM((D, H), BF16),
            pltpu.VMEM((D, H), BF16),
            slots(), slots(), slots(), slots(),
            acts(BF16), acts(BF16), acts(BF16), acts(F32), acts(F32),
            slots(), slots(), slots(), slots(),
            pltpu.VMEM((2, 3 * HALF, H), BF16),
            pltpu.VMEM((2, 3 * HALF, H), BF16),
            pltpu.VMEM((PIECES, 3 * HALF, H), BF16),
            pltpu.VMEM((PIECES, 3 * HALF, H), BF16),
            pltpu.VMEM((3 * HALF, H), F32),
            dma((5,)),
            dma((PEERS,)), dma((PEERS,)), dma((PEERS,)), dma((PEERS,)),
            dma((PEERS,)), dma((PEERS,)), dma((PEERS,)), dma((PEERS,)),
            dma((PIECES,)), dma((PIECES,)), dma((PIECES,)), dma((PIECES,)),
        ],
        compiler_params=pltpu.CompilerParams(
            collective_id=0, has_side_effects=True, vmem_limit_bytes=62 * 2**20
        ),
        name="expert_layer",
    )(expert_ids.T, gate_probs.T, tokens, out_grad, w_gate, w_up, w_down)


def solution(mesh):
    placed = (
        P(("dp", "expert"), None),
        P(("dp", "expert"), None),
        P(("dp", "expert"), None),
        P("expert", None, None),
        P("expert", None, None),
        P("expert", None, None),
        P(("dp", "expert"), None),
    )
    return jax.shard_map(
        local,
        mesh=mesh,
        in_specs=placed,
        out_specs=(
            P(("dp", "expert"), None),
            P(("dp", "expert"), None),
            P("expert", "dp", None),
            P("expert", "dp", None),
            P("expert", "dp", None),
        ),
        check_vma=False,
    )
```

```python
import functools

import jax
import jax.numpy as jnp
from jax import lax
from jax.experimental import pallas as pl
from jax.experimental.pallas import tpu as pltpu
from jax.sharding import PartitionSpec as P

MESH = pl.DeviceIdType.MESH
F32 = jnp.float32
BF16 = jnp.bfloat16

NX, NY, NC = 4, 4, 2
CHIPS = NX * NY
PEERS = CHIPS * NC
NZ = 8
TOK = 128
TOP = 2
CAP = 16
SLOTS = PEERS * CAP
D = 2048
H = 768
SHARD = D // NZ
HALF = SHARD // 2
PIECES = 7


def dot(a, b):
    return jnp.dot(a, b, preferred_element_type=F32)


def dot_rhs_t(a, b):
    return lax.dot_general(a, b, (((1,), (1,)), ((), ())), preferred_element_type=F32)


def place(index):
    return index // (NY * NC), lax.rem(index // NC, NY), lax.rem(index, NC)


def offset(j, core):
    p = lax.rem(j * 7, CHIPS)
    a, b = p // NY, lax.rem(p, NY)
    return a + core * (b - a), b + core * (a - b)


def ahead(x, y, own_core, core, j):
    dx, dy = offset(j, own_core)
    return (lax.rem(x + dx, NX) * NY + lax.rem(y + dy, NY)) * NC + core


def behind(x, y, core, j):
    dx, dy = offset(j, core)
    return (lax.rem(x + NX - dx, NX) * NY + lax.rem(y + NY - dy, NY)) * NC + core


def rows_of(block):
    return pl.ds(pl.multiple_of(block * CAP, CAP), CAP)


def loop(low, high, body):
    def step(i, carry):
        body(i)
        return carry

    lax.fori_loop(low, high, step, 0)


def kernel(
    ids_ref, prob_ref, tok_hbm, og_hbm, wg_hbm, wu_hbm, wd_hbm,
    mixed_hbm, tgrad_hbm, gg_hbm, gu_hbm, gd_hbm,
    tok, og, wg, wu, wd,
    xs, ds, xr, dr, hid, dg, du, ca, cb,
    ov, dxv, orv, dxr,
    sp, sq, rp, rq, acc, mixed, tgrad, grads,
    load_sem, store_sem, xss, dss, oss, dxss, xrs, drs, ors, dxrs, pss, qss, prs, qrs,
):
    me = lax.axis_index("expert")
    z = lax.axis_index("dp")
    x, y, core = place(me)
    up = lax.rem(z + 1, NZ)
    down = lax.rem(z + NZ - 1, NZ)

    loads = [
        pltpu.make_async_copy(src, dst, load_sem.at[i])
        for i, (src, dst) in enumerate(
            [(tok_hbm, tok), (og_hbm, og), (wg_hbm.at[0], wg), (wu_hbm.at[0], wu), (wd_hbm.at[0], wd)]
        )
    ]
    for load in loads:
        load.start()

    barrier = pltpu.get_barrier_semaphore()

    def greet(i):
        pl.semaphore_signal(
            barrier, inc=1, device_id={"expert": lax.rem(me + i, PEERS)}, device_id_type=MESH
        )

    loop(1, PEERS, greet)
    for other in (up, down):
        pl.semaphore_signal(barrier, inc=1, device_id={"dp": other}, device_id_type=MESH)

    sub = lax.broadcasted_iota(jnp.int32, (TOK, TOK), 0)
    lane = lax.broadcasted_iota(jnp.int32, (TOK, TOK), 1)
    eye = sub == lane
    lane_f = lane.astype(F32)

    def to_col(row):
        return jnp.sum(jnp.where(eye, row, 0.0), axis=1, keepdims=True)

    def to_row(col):
        return jnp.sum(jnp.where(eye, col, 0.0), axis=0, keepdims=True)

    ids_f = ids_ref[...].astype(F32)
    probs = prob_ref[...]
    id_col = [to_col(ids_f[k : k + 1]) for k in range(TOP)]
    hot = [lane_f == id_col[k] for k in range(TOP)]
    chosen = jnp.where(hot[0] | hot[1], 1.0, 0.0).astype(BF16)
    earlier = jnp.where(lane < sub, 1.0, 0.0).astype(BF16)
    before = dot(earlier, chosen)
    slot_col = [
        id_col[k] * CAP + jnp.sum(jnp.where(hot[k], before, 0.0), axis=1, keepdims=True)
        for k in range(TOP)
    ]
    slot_row = [to_row(slot_col[k]) for k in range(TOP)]
    prob_row = [probs[k : k + 1] for k in range(TOP)]
    prob_col = [to_col(prob_row[k]) for k in range(TOP)]
    slot_of = lax.broadcasted_iota(jnp.int32, (SLOTS, TOK), 0).astype(F32)
    owner = [slot_of == slot_row[k] for k in range(TOP)]
    pick = jnp.where(owner[0] | owner[1], 1.0, 0.0).astype(BF16)
    slot_prob = jnp.sum(
        jnp.where(owner[0], prob_row[0], 0.0) + jnp.where(owner[1], prob_row[1], 0.0),
        axis=1,
        keepdims=True,
    )

    WIDE = 512

    def wide(n):
        return pl.ds(pl.multiple_of(n * WIDE, WIDE), WIDE)

    loads[0].wait()

    def build_x(n):
        xs[:, wide(n)] = dot(pick, tok[:, wide(n)]).astype(BF16)

    loop(0, D // WIDE, build_x)
    pl.semaphore_wait(barrier, PEERS - 1 + 2)

    def to_expert(src, dst, send_sem, recv_sem, j, t):
        peer = ahead(x, y, core, t, j)
        return pltpu.make_async_remote_copy(
            src.at[rows_of(peer)],
            dst.at[rows_of(j * NC + core)],
            send_sem.at[t * CHIPS + j],
            recv_sem.at[j * NC + core],
            device_id={"expert": peer},
            device_id_type=MESH,
        )

    def own_block(src, dst, recv_sem):
        return pltpu.make_async_copy(src.at[rows_of(me)], dst.at[rows_of(core)], recv_sem.at[core])

    def dispatch(src, dst, send_sem, recv_sem, t):
        @pl.when(core == t)
        def _():
            own_block(src, dst, recv_sem).start()

        @pl.when(core != t)
        def _():
            to_expert(src, dst, send_sem, recv_sem, 0, t).start()

        loop(1, CHIPS, lambda j: to_expert(src, dst, send_sem, recv_sem, j, t).start())

    dispatch(xs, xr, xss, xrs, 0)
    loads[1].wait()

    def build_dy(n):
        ds[:, wide(n)] = (dot(pick, og[:, wide(n)]) * slot_prob).astype(BF16)

    loop(0, D // WIDE, build_dy)
    dispatch(ds, dr, dss, drs, 0)
    dispatch(xs, xr, xss, xrs, 1)
    dispatch(ds, dr, dss, drs, 1)

    def arrived(dst, recv_sem, i):
        pltpu.make_async_copy(dst.at[rows_of(i)], dst.at[rows_of(i)], recv_sem.at[i]).wait()

    TILE = 256
    MX = 256

    def tile(n):
        return pl.ds(pl.multiple_of(n * TILE, TILE), TILE)

    loads[2].wait()
    loads[3].wait()

    def forward(m):
        loop(0, MX // CAP, lambda i: arrived(xr, xrs, m * (MX // CAP) + i))
        rows = pl.ds(pl.multiple_of(m * MX, MX), MX)

        def columns(n):
            g = dot(xr[rows, :], wg[:, tile(n)])
            u = dot(xr[rows, :], wu[:, tile(n)])
            s = 1.0 / (1.0 + jnp.exp(-g))
            gs = g * s
            hid[rows, tile(n)] = (gs * u).astype(BF16)
            cb[rows, tile(n)] = gs
            ca[rows, tile(n)] = u * s * (1.0 + g * (1.0 - s))

        loop(0, H // TILE, columns)

    loop(0, SLOTS // MX, forward)

    loads[4].wait()
    MD = 128

    def backward(m):
        loop(0, MD // CAP, lambda i: arrived(dr, drs, m * (MD // CAP) + i))
        rows = pl.ds(pl.multiple_of(m * MD, MD), MD)

        def columns(n):
            dh = dot(dr[rows, :], wd[:, tile(n)])
            dg[rows, tile(n)] = (dh * ca[rows, tile(n)]).astype(BF16)
            du[rows, tile(n)] = (dh * cb[rows, tile(n)]).astype(BF16)

        loop(0, H // TILE, columns)

    loop(0, SLOTS // MD, backward)

    right_sides = (dg, du, hid)

    def left_sides(shard, half):
        cols = pl.ds(pl.multiple_of(shard * SHARD + half * HALF, HALF), HALF)
        xt = jnp.transpose(xr[:, cols])
        dt = jnp.transpose(dr[:, cols])
        return xt, xt, dt

    def shard_up(k):
        return lax.rem(z + 4 - (k + 1) // 2 + NZ, NZ), lax.rem(k + 1, 2)

    def shard_down(k):
        return lax.rem(z - 4 + (k + 1) // 2 + NZ, NZ), lax.rem(k, 2)

    def third(w):
        return pl.ds(w * HALF, HALF)

    def pass_on(src, slot, dst, send_sem, recv_sem, k, w, to):
        return pltpu.make_async_remote_copy(
            src.at[slot, third(w)],
            dst.at[k, third(w)],
            send_sem.at[k * 3 + w],
            recv_sem.at[k * 3 + w],
            device_id={"dp": to},
            device_id_type=MESH,
        )

    ways = (
        (shard_up, sp, rp, pss, prs, up),
        (shard_down, sq, rq, qss, qrs, down),
    )

    def first(k):
        lefts = [left_sides(*way[0](k)) for way in ways]
        for w in range(3):
            for left, (_, staged, got, send_sem, recv_sem, to) in zip(lefts, ways):
                staged[k, third(w)] = dot(left[w], right_sides[w][...]).astype(BF16)
                pass_on(staged, k, got, send_sem, recv_sem, k, w, to).start()

    loop(0, 2, first)

    def to_token(src, dst, send_sem, recv_sem, i):
        j, c = i // NC, lax.rem(i, NC)
        peer = behind(x, y, c, j)
        return pltpu.make_async_remote_copy(
            src.at[rows_of(i)],
            dst.at[rows_of(me)],
            send_sem.at[i],
            recv_sem.at[me],
            device_id={"expert": peer},
            device_id_type=MESH,
        )

    def give_back(src, dst, send_sem, recv_sem, i):
        @pl.when(i == core)
        def _():
            pltpu.make_async_copy(src.at[rows_of(i)], dst.at[rows_of(me)], recv_sem.at[me]).start()

        @pl.when(i != core)
        def _():
            to_token(src, dst, send_sem, recv_sem, i).start()

    def outputs(m):
        rows = pl.ds(pl.multiple_of(m * MD, MD), MD)

        def columns(n):
            ov[rows, tile(n)] = dot_rhs_t(hid[rows, :], wd[tile(n), :]).astype(BF16)
            dxv[rows, tile(n)] = (
                dot_rhs_t(dg[rows, :], wg[tile(n), :]) + dot_rhs_t(du[rows, :], wu[tile(n), :])
            ).astype(BF16)

        loop(0, D // TILE, columns)

        def send(i):
            give_back(ov, orv, oss, ors, m * (MD // CAP) + i)
            give_back(dxv, dxr, dxss, dxrs, m * (MD // CAP) + i)

        loop(0, MD // CAP, send)

    def later(k):
        lefts = [left_sides(*way[0](k)) for way in ways]
        for w in range(3):
            for left, (_, staged, got, send_sem, recv_sem, to) in zip(lefts, ways):
                part = dot(left[w], right_sides[w][...])
                pass_on(got, k - 2, got, send_sem, recv_sem, k - 2, w, to).wait_recv()
                got[k - 2, third(w)] = (part + got[k - 2, third(w)].astype(F32)).astype(BF16)
                pass_on(got, k - 2, got, send_sem, recv_sem, k, w, to).start()

    def outputs_and_later(k):
        outputs(k - 2)
        later(k)

    loop(2, 2 + SLOTS // MD, outputs_and_later)
    loop(2 + SLOTS // MD, PIECES, later)

    loop(0, PEERS, lambda i: arrived(orv, ors, i))
    loop(0, PEERS, lambda i: arrived(dxr, dxrs, i))
    slot_lane = lax.broadcasted_iota(jnp.int32, (TOK, SLOTS), 1).astype(F32)
    route = [slot_lane == slot_col[k] for k in range(TOP)]
    one = [jnp.where(route[k], 1.0, 0.0).astype(BF16) for k in range(TOP)]
    either = jnp.where(route[0] | route[1], 1.0, 0.0).astype(BF16)

    def combine(n):
        mixed[:, wide(n)] = (
            dot(one[0], orv[:, wide(n)]) * prob_col[0] + dot(one[1], orv[:, wide(n)]) * prob_col[1]
        ).astype(BF16)
        tgrad[:, wide(n)] = dot(either, dxr[:, wide(n)]).astype(BF16)

    loop(0, D // WIDE, combine)
    stores = [
        pltpu.make_async_copy(mixed, mixed_hbm, store_sem.at[0]),
        pltpu.make_async_copy(tgrad, tgrad_hbm, store_sem.at[1]),
    ]
    for store in stores:
        store.start()

    for half in range(2):
        left = left_sides(z, half)
        for w in range(3):
            acc[half, third(w)] = dot(left[w], right_sides[w][...])
    for w, out in enumerate((gg_hbm, gu_hbm, gd_hbm)):
        for k in (PIECES - 2, PIECES - 1):
            pass_on(rp, k, rp, pss, prs, k, w, up).wait_recv()
            pass_on(rq, k, rq, qss, qrs, k, w, down).wait_recv()
        for half, (k_up, k_down) in enumerate(((5, 6), (6, 5))):
            grads[w, half * HALF : (half + 1) * HALF] = (
                acc[half, third(w)] + rp[k_up, third(w)].astype(F32) + rq[k_down, third(w)].astype(F32)
            ).astype(BF16)
        store = pltpu.make_async_copy(grads.at[w], out.at[0], store_sem.at[2 + w])
        store.start()
        stores.append(store)

    def sent(src, dst, send_sem, recv_sem, i):
        to_expert(src, dst, send_sem, recv_sem, lax.rem(i, CHIPS), i // CHIPS).wait_send()

    def all_sent(i):
        @pl.when(i != core * CHIPS)
        def _():
            sent(xs, xr, xss, xrs, i)
            sent(ds, dr, dss, drs, i)

        @pl.when(i != core)
        def _():
            to_token(ov, orv, oss, ors, i).wait_send()
            to_token(dxv, dxr, dxss, dxrs, i).wait_send()

    loop(0, PEERS, all_sent)

    def passed(k):
        for w in range(3):
            pass_on(rp, k, rp, pss, prs, k, w, up).wait_send()
            pass_on(rq, k, rq, qss, qrs, k, w, down).wait_send()

    loop(0, PIECES, passed)
    for store in stores:
        store.wait()


def hand_on(*refs):
    count = (len(refs) - 2) // 3
    srcs, dsts, bufs = (refs[i * count : (i + 1) * count] for i in range(3))
    in_sem, out_sem = refs[3 * count :]
    ins = [pltpu.make_async_copy(s, b, in_sem.at[i]) for i, (s, b) in enumerate(zip(srcs, bufs))]
    outs = [pltpu.make_async_copy(b, d, out_sem.at[i]) for i, (b, d) in enumerate(zip(bufs, dsts))]
    for copy in ins:
        copy.start()
    for copy, then in zip(ins, outs):
        copy.wait()
        then.start()
    for copy in outs:
        copy.wait()


def local(tokens, expert_ids, gate_probs, w_gate, w_up, w_down, out_grad):
    vmem = pl.BlockSpec(memory_space=pltpu.VMEM)
    hbm = pl.BlockSpec(memory_space=pl.ANY)
    dma = pltpu.SemaphoreType.DMA
    slots = lambda: pltpu.VMEM((SLOTS, D), BF16)
    acts = lambda dtype: pltpu.VMEM((SLOTS, H), dtype)
    shapes = (
        jax.ShapeDtypeStruct((TOK, D), BF16),
        jax.ShapeDtypeStruct((TOK, D), BF16),
        jax.ShapeDtypeStruct((1, SHARD, H), BF16),
        jax.ShapeDtypeStruct((1, SHARD, H), BF16),
        jax.ShapeDtypeStruct((1, SHARD, H), BF16),
    )
    results = pl.pallas_call(
        kernel,
        out_shape=shapes,
        in_specs=[vmem, vmem] + [hbm] * 5,
        out_specs=(hbm,) * 5,
        scratch_shapes=[
            pltpu.VMEM((TOK, D), BF16),
            pltpu.VMEM((TOK, D), BF16),
            pltpu.VMEM((D, H), BF16),
            pltpu.VMEM((D, H), BF16),
            pltpu.VMEM((D, H), BF16),
            slots(), slots(), slots(), slots(),
            acts(BF16), acts(BF16), acts(BF16), acts(F32), acts(F32),
            slots(), slots(), slots(), slots(),
            pltpu.VMEM((2, 3 * HALF, H), BF16),
            pltpu.VMEM((2, 3 * HALF, H), BF16),
            pltpu.VMEM((PIECES, 3 * HALF, H), BF16),
            pltpu.VMEM((PIECES, 3 * HALF, H), BF16),
            pltpu.VMEM((2, 3 * HALF, H), F32),
            pltpu.VMEM((TOK, D), BF16),
            pltpu.VMEM((TOK, D), BF16),
            pltpu.VMEM((3, SHARD, H), BF16),
            dma((5,)), dma((5,)),
            dma((PEERS,)), dma((PEERS,)), dma((PEERS,)), dma((PEERS,)),
            dma((PEERS,)), dma((PEERS,)), dma((PEERS,)), dma((PEERS,)),
            dma((PIECES * 3,)), dma((PIECES * 3,)), dma((PIECES * 3,)), dma((PIECES * 3,)),
        ],
        compiler_params=pltpu.CompilerParams(
            collective_id=0, has_side_effects=True, vmem_limit_bytes=62 * 2**20
        ),
        name="expert_layer",
    )(expert_ids.T, gate_probs.T, tokens, out_grad, w_gate, w_up, w_down)
    return pl.pallas_call(
        hand_on,
        out_shape=shapes,
        in_specs=[hbm] * 5,
        out_specs=(hbm,) * 5,
        scratch_shapes=[pltpu.VMEM(shape.shape, shape.dtype) for shape in shapes] + [dma((5,)), dma((5,))],
        name="hand_on",
    )(*results)


def solution(mesh):
    placed = (
        P(("dp", "expert"), None),
        P(("dp", "expert"), None),
        P(("dp", "expert"), None),
        P("expert", None, None),
        P("expert", None, None),
        P("expert", None, None),
        P(("dp", "expert"), None),
    )
    return jax.shard_map(
        local,
        mesh=mesh,
        in_specs=placed,
        out_specs=(
            P(("dp", "expert"), None),
            P(("dp", "expert"), None),
            P("expert", "dp", None),
            P("expert", "dp", None),
            P("expert", "dp", None),
        ),
        check_vma=False,
    )
```

```python
import functools

import jax
import jax.numpy as jnp
from jax import lax
from jax.experimental import pallas as pl
from jax.experimental.pallas import tpu as pltpu
from jax.sharding import PartitionSpec as P

MESH = pl.DeviceIdType.MESH
F32 = jnp.float32
BF16 = jnp.bfloat16

NX, NY, NC = 4, 4, 2
CHIPS = NX * NY
OWN = CHIPS - 1
PEERS = CHIPS * NC
NZ = 8
TOK = 128
TOP = 2
CAP = 16
SLOTS = PEERS * CAP
D = 2048
H = 768
SHARD = D // NZ
HALF = SHARD // 2
PIECES = 7
SLICES = 4


def dot(a, b):
    return jnp.dot(a, b, preferred_element_type=F32)


def dot_rhs_t(a, b):
    return lax.dot_general(a, b, (((1,), (1,)), ((), ())), preferred_element_type=F32)


def place(index):
    return index // (NY * NC), lax.rem(index // NC, NY), lax.rem(index, NC)


def far_first(v):
    return 2 - v + 3 * (v // 2) - 2 * (v // 3)


def offset(j, core):
    a, b = far_first(j // NY), far_first(lax.rem(j, NY))
    return a + core * (b - a), b + core * (a - b)


def ahead(x, y, own_core, core, j):
    dx, dy = offset(j, own_core)
    return (lax.rem(x + dx, NX) * NY + lax.rem(y + dy, NY)) * NC + core


def behind(x, y, core, j):
    dx, dy = offset(j, core)
    return (lax.rem(x + NX - dx, NX) * NY + lax.rem(y + NY - dy, NY)) * NC + core


def rows_of(block):
    return pl.ds(pl.multiple_of(block * CAP, CAP), CAP)


def loop(low, high, body):
    def step(i, carry):
        body(i)
        return carry

    lax.fori_loop(low, high, step, 0)


def kernel(
    ids_hbm, prob_hbm, tok_hbm, og_hbm, wg_hbm, wu_hbm, wd_hbm,
    mixed_hbm, tgrad_hbm, gg_hbm, gu_hbm, gd_hbm,
    ids_ref, prob_ref, tok, og, wg, wu, wd,
    xs, ds, xr, dr, hid, dg, du, ca, cb,
    ov, dxv, orv, dxr,
    sp, sq, rp, rq, acc, mixed, tgrad, grads,
    load_sem, store_sem, xss, dss, oss, dxss, xrs, drs, ors, dxrs, pss, qss, prs, qrs,
):
    me = lax.axis_index("expert")
    z = lax.axis_index("dp")
    x, y, core = place(me)
    up = lax.rem(z + 1, NZ)
    down = lax.rem(z + NZ - 1, NZ)

    loads = [
        pltpu.make_async_copy(src, dst, load_sem.at[i])
        for i, (src, dst) in enumerate(
            [
                (ids_hbm, ids_ref), (prob_hbm, prob_ref), (tok_hbm, tok), (og_hbm, og),
                (wg_hbm.at[0], wg), (wu_hbm.at[0], wu), (wd_hbm.at[0], wd),
            ]
        )
    ]
    for load in loads[:4]:
        load.start()

    barrier = pltpu.get_barrier_semaphore()

    def greet(i):
        pl.semaphore_signal(
            barrier, inc=1, device_id={"expert": lax.rem(me + i, PEERS)}, device_id_type=MESH
        )

    loop(1, PEERS, greet)
    for other in (up, down):
        pl.semaphore_signal(barrier, inc=1, device_id={"dp": other}, device_id_type=MESH)

    loads[0].wait()
    loads[1].wait()

    sub = lax.broadcasted_iota(jnp.int32, (TOK, TOK), 0)
    lane = lax.broadcasted_iota(jnp.int32, (TOK, TOK), 1)
    eye = sub == lane
    lane_f = lane.astype(F32)

    def to_col(row):
        return jnp.sum(jnp.where(eye, row, 0.0), axis=1, keepdims=True)

    def to_row(col):
        return jnp.sum(jnp.where(eye, col, 0.0), axis=0, keepdims=True)

    ids_f = ids_ref[...].astype(F32)
    probs = prob_ref[...]
    id_col = [to_col(ids_f[k : k + 1]) for k in range(TOP)]
    hot = [lane_f == id_col[k] for k in range(TOP)]
    chosen = jnp.where(hot[0] | hot[1], 1.0, 0.0).astype(BF16)
    earlier = jnp.where(lane < sub, 1.0, 0.0).astype(BF16)
    before = dot(earlier, chosen)
    slot_col = [
        id_col[k] * CAP + jnp.sum(jnp.where(hot[k], before, 0.0), axis=1, keepdims=True)
        for k in range(TOP)
    ]
    slot_row = [to_row(slot_col[k]) for k in range(TOP)]
    prob_row = [probs[k : k + 1] for k in range(TOP)]
    prob_col = [to_col(prob_row[k]) for k in range(TOP)]
    slot_of = lax.broadcasted_iota(jnp.int32, (SLOTS, TOK), 0).astype(F32)
    owner = [slot_of == slot_row[k] for k in range(TOP)]
    pick = jnp.where(owner[0] | owner[1], 1.0, 0.0).astype(BF16)
    slot_prob = jnp.sum(
        jnp.where(owner[0], prob_row[0], 0.0) + jnp.where(owner[1], prob_row[1], 0.0),
        axis=1,
        keepdims=True,
    )

    WIDE = 512

    def wide(n):
        return pl.ds(pl.multiple_of(n * WIDE, WIDE), WIDE)

    loads[2].wait()

    def build_x(n):
        xs[:, wide(n)] = dot(pick, tok[:, wide(n)]).astype(BF16)

    loop(0, D // WIDE, build_x)
    for load in loads[4:]:
        load.start()
    pl.semaphore_wait(barrier, PEERS - 1 + 2)

    def to_expert(src, dst, send_sem, recv_sem, j, t):
        peer = ahead(x, y, core, t, j)
        return pltpu.make_async_remote_copy(
            src.at[rows_of(peer)],
            dst.at[rows_of(j * NC + core)],
            send_sem.at[t * CHIPS + j],
            recv_sem.at[j * NC + core],
            device_id={"expert": peer},
            device_id_type=MESH,
        )

    def own_block(src, dst, recv_sem):
        return pltpu.make_async_copy(
            src.at[rows_of(me)], dst.at[rows_of(OWN * NC + core)], recv_sem.at[OWN * NC + core]
        )

    def dispatch(src, dst, send_sem, recv_sem, t):
        loop(0, OWN, lambda j: to_expert(src, dst, send_sem, recv_sem, j, t).start())

        @pl.when(core == t)
        def _():
            own_block(src, dst, recv_sem).start()

        @pl.when(core != t)
        def _():
            to_expert(src, dst, send_sem, recv_sem, OWN, t).start()

    dispatch(xs, xr, xss, xrs, 0)
    loads[3].wait()

    def build_dy(n):
        ds[:, wide(n)] = (dot(pick, og[:, wide(n)]) * slot_prob).astype(BF16)

    loop(0, D // WIDE, build_dy)
    dispatch(ds, dr, dss, drs, 0)
    dispatch(xs, xr, xss, xrs, 1)
    dispatch(ds, dr, dss, drs, 1)

    def arrived(dst, recv_sem, i):
        pltpu.make_async_copy(dst.at[rows_of(i)], dst.at[rows_of(i)], recv_sem.at[i]).wait()

    TILE = 256
    MX = 256

    def tile(n):
        return pl.ds(pl.multiple_of(n * TILE, TILE), TILE)

    loads[4].wait()
    loads[5].wait()

    def forward(m):
        loop(0, MX // CAP, lambda i: arrived(xr, xrs, m * (MX // CAP) + i))
        rows = pl.ds(pl.multiple_of(m * MX, MX), MX)

        def columns(n):
            g = dot(xr[rows, :], wg[:, tile(n)])
            u = dot(xr[rows, :], wu[:, tile(n)])
            s = 1.0 / (1.0 + jnp.exp(-g))
            gs = g * s
            hid[rows, tile(n)] = (gs * u).astype(BF16)
            cb[rows, tile(n)] = gs
            ca[rows, tile(n)] = u * s * (1.0 + g * (1.0 - s))

        loop(0, H // TILE, columns)

    loop(0, SLOTS // MX, forward)

    loads[6].wait()
    MD = 128

    def backward(m):
        loop(0, MD // CAP, lambda i: arrived(dr, drs, m * (MD // CAP) + i))
        rows = pl.ds(pl.multiple_of(m * MD, MD), MD)

        def columns(n):
            dh = dot(dr[rows, :], wd[:, tile(n)])
            dg[rows, tile(n)] = (dh * ca[rows, tile(n)]).astype(BF16)
            du[rows, tile(n)] = (dh * cb[rows, tile(n)]).astype(BF16)

        loop(0, H // TILE, columns)

    loop(0, SLOTS // MD, backward)

    right_sides = (dg, du, hid)

    def part(shard, half, w, kept):
        cols = pl.ds(pl.multiple_of(shard * SHARD + half * HALF, HALF), HALF)
        if w == 0:
            kept[:] = [jnp.transpose(xr[:, cols])]
        if w == 2:
            kept[:] = [jnp.transpose(dr[:, cols])]
        return dot(kept[0], right_sides[w][...])

    def shard_up(k):
        return lax.rem(z + 4 - (k + 1) // 2 + NZ, NZ), lax.rem(k + 1, 2)

    def shard_down(k):
        return lax.rem(z - 4 + (k + 1) // 2 + NZ, NZ), lax.rem(k, 2)

    def third(w):
        return pl.ds(w * HALF, HALF)

    def pass_on(src, slot, dst, send_sem, recv_sem, k, w, to):
        return pltpu.make_async_remote_copy(
            src.at[slot, third(w)],
            dst.at[k, third(w)],
            send_sem.at[k * 3 + w],
            recv_sem.at[k * 3 + w],
            device_id={"dp": to},
            device_id_type=MESH,
        )

    ways = (
        (shard_up, sp, rp, pss, prs, up),
        (shard_down, sq, rq, qss, qrs, down),
    )

    def first(k):
        kept = [[], []]
        for w in range(3):
            for left, (which, staged, got, send_sem, recv_sem, to) in zip(kept, ways):
                staged[k, third(w)] = part(*which(k), w, left).astype(BF16)
                pass_on(staged, k, got, send_sem, recv_sem, k, w, to).start()

    loop(0, 2, first)

    def to_token(src, dst, send_sem, recv_sem, i):
        j, c = i // NC, lax.rem(i, NC)
        peer = behind(x, y, c, j)
        return pltpu.make_async_remote_copy(
            src.at[rows_of(i)],
            dst.at[rows_of(me)],
            send_sem.at[i],
            recv_sem.at[me],
            device_id={"expert": peer},
            device_id_type=MESH,
        )

    def give_back(src, dst, send_sem, recv_sem, i):
        @pl.when(i == OWN * NC + core)
        def _():
            pltpu.make_async_copy(src.at[rows_of(i)], dst.at[rows_of(me)], recv_sem.at[me]).start()

        @pl.when(i != OWN * NC + core)
        def _():
            to_token(src, dst, send_sem, recv_sem, i).start()

    def outputs(m):
        rows = pl.ds(pl.multiple_of(m * MD, MD), MD)

        def columns(n):
            ov[rows, tile(n)] = dot_rhs_t(hid[rows, :], wd[tile(n), :]).astype(BF16)
            dxv[rows, tile(n)] = (
                dot_rhs_t(dg[rows, :], wg[tile(n), :]) + dot_rhs_t(du[rows, :], wu[tile(n), :])
            ).astype(BF16)

        loop(0, D // TILE, columns)

        def send(i):
            give_back(ov, orv, oss, ors, m * (MD // CAP) + i)
            give_back(dxv, dxr, dxss, dxrs, m * (MD // CAP) + i)

        loop(0, MD // CAP, send)

    def later(k):
        kept = [[], []]
        for w in range(3):
            for left, (which, staged, got, send_sem, recv_sem, to) in zip(kept, ways):
                mine = part(*which(k), w, left)
                pass_on(got, k - 2, got, send_sem, recv_sem, k - 2, w, to).wait_recv()
                got[k - 2, third(w)] = (mine + got[k - 2, third(w)].astype(F32)).astype(BF16)
                pass_on(got, k - 2, got, send_sem, recv_sem, k, w, to).start()

    def outputs_and_later(k):
        outputs(k - 2)
        later(k)

    loop(2, 2 + SLOTS // MD, outputs_and_later)
    loop(2 + SLOTS // MD, PIECES, later)

    loop(0, PEERS, lambda i: arrived(orv, ors, i))
    loop(0, PEERS, lambda i: arrived(dxr, dxrs, i))
    slot_lane = lax.broadcasted_iota(jnp.int32, (TOK, SLOTS), 1).astype(F32)
    route = [slot_lane == slot_col[k] for k in range(TOP)]
    one = [jnp.where(route[k], 1.0, 0.0).astype(BF16) for k in range(TOP)]
    either = jnp.where(route[0] | route[1], 1.0, 0.0).astype(BF16)

    def combine(n):
        mixed[:, wide(n)] = (
            dot(one[0], orv[:, wide(n)]) * prob_col[0] + dot(one[1], orv[:, wide(n)]) * prob_col[1]
        ).astype(BF16)
        tgrad[:, wide(n)] = dot(either, dxr[:, wide(n)]).astype(BF16)

    loop(0, D // WIDE, combine)
    stores = [
        pltpu.make_async_copy(mixed, mixed_hbm, store_sem.at[0]),
        pltpu.make_async_copy(tgrad, tgrad_hbm, store_sem.at[1]),
    ]
    for store in stores:
        store.start()

    for half in range(2):
        left = []
        for w in range(3):
            acc[half, third(w)] = part(z, half, w, left)
    for w, out in enumerate((gg_hbm, gu_hbm, gd_hbm)):
        for k in (PIECES - 2, PIECES - 1):
            pass_on(rp, k, rp, pss, prs, k, w, up).wait_recv()
            pass_on(rq, k, rq, qss, qrs, k, w, down).wait_recv()
        for half, (k_up, k_down) in enumerate(((5, 6), (6, 5))):
            grads[w, half * HALF : (half + 1) * HALF] = (
                acc[half, third(w)] + rp[k_up, third(w)].astype(F32) + rq[k_down, third(w)].astype(F32)
            ).astype(BF16)
        store = pltpu.make_async_copy(grads.at[w], out.at[0], store_sem.at[2 + w])
        store.start()
        stores.append(store)

    def sent(src, dst, send_sem, recv_sem, i):
        to_expert(src, dst, send_sem, recv_sem, lax.rem(i, CHIPS), i // CHIPS).wait_send()

    def all_sent(i):
        @pl.when(i != core * CHIPS + OWN)
        def _():
            sent(xs, xr, xss, xrs, i)
            sent(ds, dr, dss, drs, i)

        @pl.when(i != OWN * NC + core)
        def _():
            to_token(ov, orv, oss, ors, i).wait_send()
            to_token(dxv, dxr, dxss, dxrs, i).wait_send()

    loop(0, PEERS, all_sent)

    def passed(k):
        for w in range(3):
            pass_on(rp, k, rp, pss, prs, k, w, up).wait_send()
            pass_on(rq, k, rq, qss, qrs, k, w, down).wait_send()

    loop(0, PIECES, passed)
    for store in stores:
        store.wait()


def hand_on(*refs):
    count = (len(refs) - 2) // 3
    arrays = [refs[i * count : (i + 1) * count] for i in range(3)]
    in_sem, out_sem = refs[3 * count :]
    pieces = []
    for array in zip(*arrays):
        rows = array[0].shape[-2] // SLICES
        for i in range(SLICES):
            at = (0,) * (len(array[0].shape) - 2) + (pl.ds(i * rows, rows),)
            pieces.append([ref.at[at] for ref in array])
    ins = [pltpu.make_async_copy(s, b, in_sem.at[i]) for i, (s, d, b) in enumerate(pieces)]
    outs = [pltpu.make_async_copy(b, d, out_sem.at[i]) for i, (s, d, b) in enumerate(pieces)]
    for copy in ins:
        copy.start()
    for copy, then in zip(ins, outs):
        copy.wait()
        then.start()
    for copy in outs:
        copy.wait()


def local(tokens, expert_ids, gate_probs, w_gate, w_up, w_down, out_grad):
    hbm = pl.BlockSpec(memory_space=pl.ANY)
    dma = pltpu.SemaphoreType.DMA
    slots = lambda: pltpu.VMEM((SLOTS, D), BF16)
    acts = lambda dtype: pltpu.VMEM((SLOTS, H), dtype)
    shapes = (
        jax.ShapeDtypeStruct((TOK, D), BF16),
        jax.ShapeDtypeStruct((TOK, D), BF16),
        jax.ShapeDtypeStruct((1, SHARD, H), BF16),
        jax.ShapeDtypeStruct((1, SHARD, H), BF16),
        jax.ShapeDtypeStruct((1, SHARD, H), BF16),
    )
    results = pl.pallas_call(
        kernel,
        out_shape=shapes,
        in_specs=[hbm] * 7,
        out_specs=(hbm,) * 5,
        scratch_shapes=[
            pltpu.VMEM((TOP, TOK), jnp.int32),
            pltpu.VMEM((TOP, TOK), F32),
            pltpu.VMEM((TOK, D), BF16),
            pltpu.VMEM((TOK, D), BF16),
            pltpu.VMEM((D, H), BF16),
            pltpu.VMEM((D, H), BF16),
            pltpu.VMEM((D, H), BF16),
            slots(), slots(), slots(), slots(),
            acts(BF16), acts(BF16), acts(BF16), acts(F32), acts(F32),
            slots(), slots(), slots(), slots(),
            pltpu.VMEM((2, 3 * HALF, H), BF16),
            pltpu.VMEM((2, 3 * HALF, H), BF16),
            pltpu.VMEM((PIECES, 3 * HALF, H), BF16),
            pltpu.VMEM((PIECES, 3 * HALF, H), BF16),
            pltpu.VMEM((2, 3 * HALF, H), F32),
            pltpu.VMEM((TOK, D), BF16),
            pltpu.VMEM((TOK, D), BF16),
            pltpu.VMEM((3, SHARD, H), BF16),
            dma((7,)), dma((5,)),
            dma((PEERS,)), dma((PEERS,)), dma((PEERS,)), dma((PEERS,)),
            dma((PEERS,)), dma((PEERS,)), dma((PEERS,)), dma((PEERS,)),
            dma((PIECES * 3,)), dma((PIECES * 3,)), dma((PIECES * 3,)), dma((PIECES * 3,)),
        ],
        compiler_params=pltpu.CompilerParams(
            collective_id=0, has_side_effects=True, vmem_limit_bytes=62 * 2**20
        ),
        name="expert_layer",
    )(expert_ids.T, gate_probs.T, tokens, out_grad, w_gate, w_up, w_down)
    return pl.pallas_call(
        hand_on,
        out_shape=shapes,
        in_specs=[hbm] * 5,
        out_specs=(hbm,) * 5,
        scratch_shapes=[pltpu.VMEM(shape.shape, shape.dtype) for shape in shapes]
        + [dma((5 * SLICES,)), dma((5 * SLICES,))],
        name="hand_on",
    )(*results)


def solution(mesh):
    placed = (
        P(("dp", "expert"), None),
        P(("dp", "expert"), None),
        P(("dp", "expert"), None),
        P("expert", None, None),
        P("expert", None, None),
        P("expert", None, None),
        P(("dp", "expert"), None),
    )
    return jax.shard_map(
        local,
        mesh=mesh,
        in_specs=placed,
        out_specs=(
            P(("dp", "expert"), None),
            P(("dp", "expert"), None),
            P("expert", "dp", None),
            P("expert", "dp", None),
            P("expert", "dp", None),
        ),
        check_vma=False,
    )
```

```python
import functools

import jax
import jax.numpy as jnp
from jax import lax
from jax.experimental import pallas as pl
from jax.experimental.pallas import tpu as pltpu
from jax.sharding import PartitionSpec as P

MESH = pl.DeviceIdType.MESH
F32 = jnp.float32
BF16 = jnp.bfloat16

NX, NY, NC = 4, 4, 2
CHIPS = NX * NY
OWN = CHIPS - 1
PEERS = CHIPS * NC
NZ = 8
TOK = 128
TOP = 2
CAP = 16
SLOTS = PEERS * CAP
D = 2048
H = 768
SHARD = D // NZ
HALF = SHARD // 2
PIECES = 7


def dot(a, b):
    return jnp.dot(a, b, preferred_element_type=F32)


def dot_rhs_t(a, b):
    return lax.dot_general(a, b, (((1,), (1,)), ((), ())), preferred_element_type=F32)


def place(index):
    return index // (NY * NC), lax.rem(index // NC, NY), lax.rem(index, NC)


def offset(j, core):
    p = lax.rem((j + 1) * 7, CHIPS)
    a, b = p // NY, lax.rem(p, NY)
    return a + core * (b - a), b + core * (a - b)


def ahead(x, y, own_core, core, j):
    dx, dy = offset(j, own_core)
    return (lax.rem(x + dx, NX) * NY + lax.rem(y + dy, NY)) * NC + core


def behind(x, y, core, j):
    dx, dy = offset(j, core)
    return (lax.rem(x + NX - dx, NX) * NY + lax.rem(y + NY - dy, NY)) * NC + core


def rows_of(block):
    return pl.ds(pl.multiple_of(block * CAP, CAP), CAP)


def loop(low, high, body):
    def step(i, carry):
        body(i)
        return carry

    lax.fori_loop(low, high, step, 0)


def kernel(
    ids_hbm, prob_hbm, tok_hbm, og_hbm, wg_hbm, wu_hbm, wd_hbm,
    mixed_hbm, tgrad_hbm, gg_hbm, gu_hbm, gd_hbm,
    ids_ref, prob_ref, tok, og, wg, wu, wd,
    xs, ds, xr, dr, hid, dg, du, ca, cb,
    ov, dxv, orv, dxr,
    sp, sq, rp, rq, acc, mixed, tgrad, grads,
    load_sem, store_sem, xss, dss, oss, dxss, xrs, drs, ors, dxrs, pss, qss, prs, qrs, turn,
):
    me = lax.axis_index("expert")
    z = lax.axis_index("dp")
    x, y, core = place(me)
    up = lax.rem(z + 1, NZ)
    down = lax.rem(z + NZ - 1, NZ)

    loads = [
        pltpu.make_async_copy(src, dst, load_sem.at[i])
        for i, (src, dst) in enumerate(
            [
                (ids_hbm, ids_ref), (prob_hbm, prob_ref), (tok_hbm, tok), (og_hbm, og),
                (wg_hbm.at[0], wg), (wu_hbm.at[0], wu), (wd_hbm.at[0], wd),
            ]
        )
    ]
    for load in loads[:4]:
        load.start()

    barrier = pltpu.get_barrier_semaphore()

    def greet(i):
        pl.semaphore_signal(
            barrier, inc=1, device_id={"expert": lax.rem(me + i, PEERS)}, device_id_type=MESH
        )

    loop(1, PEERS, greet)
    for other in (up, down):
        pl.semaphore_signal(barrier, inc=1, device_id={"dp": other}, device_id_type=MESH)

    loads[0].wait()
    loads[1].wait()

    sub = lax.broadcasted_iota(jnp.int32, (TOK, TOK), 0)
    lane = lax.broadcasted_iota(jnp.int32, (TOK, TOK), 1)
    eye = sub == lane
    lane_f = lane.astype(F32)

    def to_col(row):
        return jnp.sum(jnp.where(eye, row, 0.0), axis=1, keepdims=True)

    def to_row(col):
        return jnp.sum(jnp.where(eye, col, 0.0), axis=0, keepdims=True)

    ids_f = ids_ref[...].astype(F32)
    probs = prob_ref[...]
    id_col = [to_col(ids_f[k : k + 1]) for k in range(TOP)]
    hot = [lane_f == id_col[k] for k in range(TOP)]
    chosen = jnp.where(hot[0] | hot[1], 1.0, 0.0).astype(BF16)
    earlier = jnp.where(lane < sub, 1.0, 0.0).astype(BF16)
    before = dot(earlier, chosen)
    slot_col = [
        id_col[k] * CAP + jnp.sum(jnp.where(hot[k], before, 0.0), axis=1, keepdims=True)
        for k in range(TOP)
    ]
    slot_row = [to_row(slot_col[k]) for k in range(TOP)]
    prob_row = [probs[k : k + 1] for k in range(TOP)]
    prob_col = [to_col(prob_row[k]) for k in range(TOP)]
    slot_of = lax.broadcasted_iota(jnp.int32, (SLOTS, TOK), 0).astype(F32)
    owner = [slot_of == slot_row[k] for k in range(TOP)]
    pick = jnp.where(owner[0] | owner[1], 1.0, 0.0).astype(BF16)
    slot_prob = jnp.sum(
        jnp.where(owner[0], prob_row[0], 0.0) + jnp.where(owner[1], prob_row[1], 0.0),
        axis=1,
        keepdims=True,
    )

    WIDE = 512

    def wide(n):
        return pl.ds(pl.multiple_of(n * WIDE, WIDE), WIDE)

    loads[2].wait()

    def build_x(n):
        xs[:, wide(n)] = dot(pick, tok[:, wide(n)]).astype(BF16)

    loop(0, D // WIDE, build_x)
    for load in loads[4:]:
        load.start()
    pl.semaphore_wait(barrier, PEERS - 1 + 2)

    def to_expert(src, dst, send_sem, recv_sem, j, t):
        peer = ahead(x, y, core, t, j)
        return pltpu.make_async_remote_copy(
            src.at[rows_of(peer)],
            dst.at[rows_of(j * NC + core)],
            send_sem.at[t * CHIPS + j],
            recv_sem.at[j * NC + core],
            device_id={"expert": peer},
            device_id_type=MESH,
        )

    def own_block(src, dst, recv_sem):
        return pltpu.make_async_copy(
            src.at[rows_of(me)], dst.at[rows_of(OWN * NC + core)], recv_sem.at[OWN * NC + core]
        )

    def dispatch(src, dst, send_sem, recv_sem, t):
        loop(0, OWN, lambda j: to_expert(src, dst, send_sem, recv_sem, j, t).start())

        @pl.when(core == t)
        def _():
            own_block(src, dst, recv_sem).start()

        @pl.when(core != t)
        def _():
            to_expert(src, dst, send_sem, recv_sem, OWN, t).start()

    dispatch(xs, xr, xss, xrs, 0)
    loads[3].wait()

    def build_dy(n):
        ds[:, wide(n)] = (dot(pick, og[:, wide(n)]) * slot_prob).astype(BF16)

    loop(0, D // WIDE, build_dy)
    dispatch(ds, dr, dss, drs, 0)

    def dispatch_second():
        dispatch(xs, xr, xss, xrs, 1)
        dispatch(ds, dr, dss, drs, 1)

    @pl.when(core == 1)
    def _():
        pl.semaphore_wait(turn, 1)
        dispatch_second()

    def arrived(dst, recv_sem, i):
        pltpu.make_async_copy(dst.at[rows_of(i)], dst.at[rows_of(i)], recv_sem.at[i]).wait()

    TILE = 256
    MX = 256

    def tile(n):
        return pl.ds(pl.multiple_of(n * TILE, TILE), TILE)

    loads[4].wait()
    loads[5].wait()

    def forward(m):
        loop(0, MX // CAP, lambda i: arrived(xr, xrs, m * (MX // CAP) + i))
        rows = pl.ds(pl.multiple_of(m * MX, MX), MX)

        def columns(n):
            g = dot(xr[rows, :], wg[:, tile(n)])
            u = dot(xr[rows, :], wu[:, tile(n)])
            s = 1.0 / (1.0 + jnp.exp(-g))
            gs = g * s
            hid[rows, tile(n)] = (gs * u).astype(BF16)
            cb[rows, tile(n)] = gs
            ca[rows, tile(n)] = u * s * (1.0 + g * (1.0 - s))

        loop(0, H // TILE, columns)

    loop(0, SLOTS // MX, forward)

    loads[6].wait()
    MD = 128

    def backward(m):
        loop(0, MD // CAP, lambda i: arrived(dr, drs, m * (MD // CAP) + i))
        rows = pl.ds(pl.multiple_of(m * MD, MD), MD)

        def columns(n):
            dh = dot(dr[rows, :], wd[:, tile(n)])
            dg[rows, tile(n)] = (dh * ca[rows, tile(n)]).astype(BF16)
            du[rows, tile(n)] = (dh * cb[rows, tile(n)]).astype(BF16)

        loop(0, H // TILE, columns)

    loop(0, SLOTS // MD, backward)

    @pl.when(core == 0)
    def _():
        pl.semaphore_signal(turn, inc=1, device_id={"expert": me + 1}, device_id_type=MESH)

    right_sides = (dg, du, hid)

    def part(shard, half, w, kept):
        cols = pl.ds(pl.multiple_of(shard * SHARD + half * HALF, HALF), HALF)
        if w == 0:
            kept[:] = [jnp.transpose(xr[:, cols])]
        if w == 2:
            kept[:] = [jnp.transpose(dr[:, cols])]
        return dot(kept[0], right_sides[w][...])

    def shard_up(k):
        return lax.rem(z + 4 - (k + 1) // 2 + NZ, NZ), lax.rem(k + 1, 2)

    def shard_down(k):
        return lax.rem(z - 4 + (k + 1) // 2 + NZ, NZ), lax.rem(k, 2)

    def third(w):
        return pl.ds(w * HALF, HALF)

    def pass_on(src, slot, dst, send_sem, recv_sem, k, w, to):
        return pltpu.make_async_remote_copy(
            src.at[slot, third(w)],
            dst.at[k, third(w)],
            send_sem.at[k * 3 + w],
            recv_sem.at[k * 3 + w],
            device_id={"dp": to},
            device_id_type=MESH,
        )

    ways = (
        (shard_up, sp, rp, pss, prs, up),
        (shard_down, sq, rq, qss, qrs, down),
    )

    def first(k):
        kept = [[], []]
        for w in range(3):
            for left, (which, staged, got, send_sem, recv_sem, to) in zip(kept, ways):
                staged[k, third(w)] = part(*which(k), w, left).astype(BF16)
                pass_on(staged, k, got, send_sem, recv_sem, k, w, to).start()

    loop(0, 2, first)

    @pl.when(core == 0)
    def _():
        dispatch_second()

    def to_token(src, dst, send_sem, recv_sem, i):
        j, c = i // NC, lax.rem(i, NC)
        peer = behind(x, y, c, j)
        return pltpu.make_async_remote_copy(
            src.at[rows_of(i)],
            dst.at[rows_of(me)],
            send_sem.at[i],
            recv_sem.at[me],
            device_id={"expert": peer},
            device_id_type=MESH,
        )

    def give_back(src, dst, send_sem, recv_sem, i):
        @pl.when(i == OWN * NC + core)
        def _():
            pltpu.make_async_copy(src.at[rows_of(i)], dst.at[rows_of(me)], recv_sem.at[me]).start()

        @pl.when(i != OWN * NC + core)
        def _():
            to_token(src, dst, send_sem, recv_sem, i).start()

    def outputs(m):
        rows = pl.ds(pl.multiple_of(m * MD, MD), MD)

        def columns(n):
            ov[rows, tile(n)] = dot_rhs_t(hid[rows, :], wd[tile(n), :]).astype(BF16)
            dxv[rows, tile(n)] = (
                dot_rhs_t(dg[rows, :], wg[tile(n), :]) + dot_rhs_t(du[rows, :], wu[tile(n), :])
            ).astype(BF16)

        loop(0, D // TILE, columns)

        def send(i):
            give_back(ov, orv, oss, ors, m * (MD // CAP) + i)
            give_back(dxv, dxr, dxss, dxrs, m * (MD // CAP) + i)

        loop(0, MD // CAP, send)

    def later(k):
        kept = [[], []]
        for w in range(3):
            for left, (which, staged, got, send_sem, recv_sem, to) in zip(kept, ways):
                mine = part(*which(k), w, left)
                pass_on(got, k - 2, got, send_sem, recv_sem, k - 2, w, to).wait_recv()
                got[k - 2, third(w)] = (mine + got[k - 2, third(w)].astype(F32)).astype(BF16)
                pass_on(got, k - 2, got, send_sem, recv_sem, k, w, to).start()

    def outputs_and_later(k):
        outputs(k - 2)
        later(k)

    loop(2, 2 + SLOTS // MD, outputs_and_later)
    loop(2 + SLOTS // MD, PIECES, later)

    loop(0, PEERS, lambda i: arrived(orv, ors, i))
    loop(0, PEERS, lambda i: arrived(dxr, dxrs, i))
    slot_lane = lax.broadcasted_iota(jnp.int32, (TOK, SLOTS), 1).astype(F32)
    route = [slot_lane == slot_col[k] for k in range(TOP)]
    one = [jnp.where(route[k], 1.0, 0.0).astype(BF16) for k in range(TOP)]
    either = jnp.where(route[0] | route[1], 1.0, 0.0).astype(BF16)

    def combine(n):
        mixed[:, wide(n)] = (
            dot(one[0], orv[:, wide(n)]) * prob_col[0] + dot(one[1], orv[:, wide(n)]) * prob_col[1]
        ).astype(BF16)
        tgrad[:, wide(n)] = dot(either, dxr[:, wide(n)]).astype(BF16)

    loop(0, D // WIDE, combine)
    stores = [
        pltpu.make_async_copy(mixed, mixed_hbm, store_sem.at[0]),
        pltpu.make_async_copy(tgrad, tgrad_hbm, store_sem.at[1]),
    ]
    for store in stores:
        store.start()

    for half in range(2):
        left = []
        for w in range(3):
            acc[half, third(w)] = part(z, half, w, left)
    for w, out in enumerate((gg_hbm, gu_hbm, gd_hbm)):
        for k in (PIECES - 2, PIECES - 1):
            pass_on(rp, k, rp, pss, prs, k, w, up).wait_recv()
            pass_on(rq, k, rq, qss, qrs, k, w, down).wait_recv()
        for half, (k_up, k_down) in enumerate(((5, 6), (6, 5))):
            grads[w, half * HALF : (half + 1) * HALF] = (
                acc[half, third(w)] + rp[k_up, third(w)].astype(F32) + rq[k_down, third(w)].astype(F32)
            ).astype(BF16)
        store = pltpu.make_async_copy(grads.at[w], out.at[0], store_sem.at[2 + w])
        store.start()
        stores.append(store)

    def sent(src, dst, send_sem, recv_sem, i):
        to_expert(src, dst, send_sem, recv_sem, lax.rem(i, CHIPS), i // CHIPS).wait_send()

    def all_sent(i):
        @pl.when(i != core * CHIPS + OWN)
        def _():
            sent(xs, xr, xss, xrs, i)
            sent(ds, dr, dss, drs, i)

        @pl.when(i != OWN * NC + core)
        def _():
            to_token(ov, orv, oss, ors, i).wait_send()
            to_token(dxv, dxr, dxss, dxrs, i).wait_send()

    loop(0, PEERS, all_sent)

    def passed(k):
        for w in range(3):
            pass_on(rp, k, rp, pss, prs, k, w, up).wait_send()
            pass_on(rq, k, rq, qss, qrs, k, w, down).wait_send()

    loop(0, PIECES, passed)
    for store in stores:
        store.wait()


def hand_on(*refs):
    count = (len(refs) - 2) // 3
    srcs, dsts, bufs = (refs[i * count : (i + 1) * count] for i in range(3))
    in_sem, out_sem = refs[3 * count :]
    ins = [pltpu.make_async_copy(s, b, in_sem.at[i]) for i, (s, b) in enumerate(zip(srcs, bufs))]
    outs = [pltpu.make_async_copy(b, d, out_sem.at[i]) for i, (b, d) in enumerate(zip(bufs, dsts))]
    for copy in ins:
        copy.start()
    for copy, then in zip(ins, outs):
        copy.wait()
        then.start()
    for copy in outs:
        copy.wait()


def local(tokens, expert_ids, gate_probs, w_gate, w_up, w_down, out_grad):
    hbm = pl.BlockSpec(memory_space=pl.ANY)
    dma = pltpu.SemaphoreType.DMA
    slots = lambda: pltpu.VMEM((SLOTS, D), BF16)
    acts = lambda dtype: pltpu.VMEM((SLOTS, H), dtype)
    shapes = (
        jax.ShapeDtypeStruct((TOK, D), BF16),
        jax.ShapeDtypeStruct((TOK, D), BF16),
        jax.ShapeDtypeStruct((1, SHARD, H), BF16),
        jax.ShapeDtypeStruct((1, SHARD, H), BF16),
        jax.ShapeDtypeStruct((1, SHARD, H), BF16),
    )
    results = pl.pallas_call(
        kernel,
        out_shape=shapes,
        in_specs=[hbm] * 7,
        out_specs=(hbm,) * 5,
        scratch_shapes=[
            pltpu.VMEM((TOP, TOK), jnp.int32),
            pltpu.VMEM((TOP, TOK), F32),
            pltpu.VMEM((TOK, D), BF16),
            pltpu.VMEM((TOK, D), BF16),
            pltpu.VMEM((D, H), BF16),
            pltpu.VMEM((D, H), BF16),
            pltpu.VMEM((D, H), BF16),
            slots(), slots(), slots(), slots(),
            acts(BF16), acts(BF16), acts(BF16), acts(F32), acts(F32),
            slots(), slots(), slots(), slots(),
            pltpu.VMEM((2, 3 * HALF, H), BF16),
            pltpu.VMEM((2, 3 * HALF, H), BF16),
            pltpu.VMEM((PIECES, 3 * HALF, H), BF16),
            pltpu.VMEM((PIECES, 3 * HALF, H), BF16),
            pltpu.VMEM((2, 3 * HALF, H), F32),
            pltpu.VMEM((TOK, D), BF16),
            pltpu.VMEM((TOK, D), BF16),
            pltpu.VMEM((3, SHARD, H), BF16),
            dma((7,)), dma((5,)),
            dma((PEERS,)), dma((PEERS,)), dma((PEERS,)), dma((PEERS,)),
            dma((PEERS,)), dma((PEERS,)), dma((PEERS,)), dma((PEERS,)),
            dma((PIECES * 3,)), dma((PIECES * 3,)), dma((PIECES * 3,)), dma((PIECES * 3,)),
            pltpu.SemaphoreType.REGULAR,
        ],
        compiler_params=pltpu.CompilerParams(
            collective_id=0, has_side_effects=True, vmem_limit_bytes=62 * 2**20
        ),
        name="expert_layer",
    )(expert_ids.T, gate_probs.T, tokens, out_grad, w_gate, w_up, w_down)
    return pl.pallas_call(
        hand_on,
        out_shape=shapes,
        in_specs=[hbm] * 5,
        out_specs=(hbm,) * 5,
        scratch_shapes=[pltpu.VMEM(shape.shape, shape.dtype) for shape in shapes] + [dma((5,)), dma((5,))],
        name="hand_on",
    )(*results)


def solution(mesh):
    placed = (
        P(("dp", "expert"), None),
        P(("dp", "expert"), None),
        P(("dp", "expert"), None),
        P("expert", None, None),
        P("expert", None, None),
        P("expert", None, None),
        P(("dp", "expert"), None),
    )
    return jax.shard_map(
        local,
        mesh=mesh,
        in_specs=placed,
        out_specs=(
            P(("dp", "expert"), None),
            P(("dp", "expert"), None),
            P("expert", "dp", None),
            P("expert", "dp", None),
            P("expert", "dp", None),
        ),
        check_vma=False,
    )
```

```python
import functools

import jax
import jax.numpy as jnp
from jax import lax
from jax.experimental import pallas as pl
from jax.experimental.pallas import tpu as pltpu
from jax.sharding import PartitionSpec as P

MESH = pl.DeviceIdType.MESH
F32 = jnp.float32
BF16 = jnp.bfloat16

NX, NY, NC = 4, 4, 2
CHIPS = NX * NY
OWN = CHIPS - 1
PEERS = CHIPS * NC
NZ = 8
TOK = 128
TOP = 2
CAP = 16
SLOTS = PEERS * CAP
D = 2048
H = 768
SHARD = D // NZ
HALF = SHARD // 2
PIECES = 7


def dot(a, b):
    return jnp.dot(a, b, preferred_element_type=F32)


def dot_rhs_t(a, b):
    return lax.dot_general(a, b, (((1,), (1,)), ((), ())), preferred_element_type=F32)


def place(index):
    return index // (NY * NC), lax.rem(index // NC, NY), lax.rem(index, NC)


def offset(j, core):
    p = lax.rem((j + 1) * 5, CHIPS)
    a, b = p // NY, lax.rem(p, NY)
    return a + core * (b - a), b + core * (a - b)


def ahead(x, y, own_core, core, j):
    dx, dy = offset(j, own_core)
    return (lax.rem(x + dx, NX) * NY + lax.rem(y + dy, NY)) * NC + core


def behind(x, y, core, j):
    dx, dy = offset(j, core)
    return (lax.rem(x + NX - dx, NX) * NY + lax.rem(y + NY - dy, NY)) * NC + core


def rows_of(block):
    return pl.ds(pl.multiple_of(block * CAP, CAP), CAP)


def loop(low, high, body):
    def step(i, carry):
        body(i)
        return carry

    lax.fori_loop(low, high, step, 0)


def kernel(
    ids_hbm, prob_hbm, tok_hbm, og_hbm, wg_hbm, wu_hbm, wd_hbm,
    mixed_hbm, tgrad_hbm, gg_hbm, gu_hbm, gd_hbm,
    ids_ref, prob_ref, tok, og, wg, wu, wd,
    xs, ds, xr, dr, hid, dg, du, ca, cb,
    ov, dxv, orv, dxr,
    sp, sq, rp, rq, acc, mixed, tgrad, grads,
    load_sem, store_sem, xss, dss, oss, dxss, xrs, drs, ors, dxrs, pss, qss, prs, qrs, turn,
):
    me = lax.axis_index("expert")
    z = lax.axis_index("dp")
    x, y, core = place(me)
    up = lax.rem(z + 1, NZ)
    down = lax.rem(z + NZ - 1, NZ)

    loads = [
        pltpu.make_async_copy(src, dst, load_sem.at[i])
        for i, (src, dst) in enumerate(
            [
                (ids_hbm, ids_ref), (prob_hbm, prob_ref), (tok_hbm, tok), (og_hbm, og),
                (wg_hbm.at[0], wg), (wu_hbm.at[0], wu), (wd_hbm.at[0], wd),
            ]
        )
    ]
    for load in loads[:4]:
        load.start()

    barrier = pltpu.get_barrier_semaphore()

    def greet(i):
        pl.semaphore_signal(
            barrier, inc=1, device_id={"expert": lax.rem(me + i, PEERS)}, device_id_type=MESH
        )

    loop(1, PEERS, greet)
    for other in (up, down):
        pl.semaphore_signal(barrier, inc=1, device_id={"dp": other}, device_id_type=MESH)

    loads[0].wait()
    loads[1].wait()

    sub = lax.broadcasted_iota(jnp.int32, (TOK, TOK), 0)
    lane = lax.broadcasted_iota(jnp.int32, (TOK, TOK), 1)
    eye = sub == lane
    lane_f = lane.astype(F32)

    def to_col(row):
        return jnp.sum(jnp.where(eye, row, 0.0), axis=1, keepdims=True)

    def to_row(col):
        return jnp.sum(jnp.where(eye, col, 0.0), axis=0, keepdims=True)

    ids_f = ids_ref[...].astype(F32)
    probs = prob_ref[...]
    id_col = [to_col(ids_f[k : k + 1]) for k in range(TOP)]
    hot = [lane_f == id_col[k] for k in range(TOP)]
    chosen = jnp.where(hot[0] | hot[1], 1.0, 0.0).astype(BF16)
    earlier = jnp.where(lane < sub, 1.0, 0.0).astype(BF16)
    before = dot(earlier, chosen)
    slot_col = [
        id_col[k] * CAP + jnp.sum(jnp.where(hot[k], before, 0.0), axis=1, keepdims=True)
        for k in range(TOP)
    ]
    slot_row = [to_row(slot_col[k]) for k in range(TOP)]
    prob_row = [probs[k : k + 1] for k in range(TOP)]
    prob_col = [to_col(prob_row[k]) for k in range(TOP)]
    row = lax.broadcasted_iota(jnp.int32, (SLOTS, TOK), 0)
    block = row // CAP
    slot_of = (((block % CHIPS) * NC + block // CHIPS) * CAP + row % CAP).astype(F32)
    owner = [slot_of == slot_row[k] for k in range(TOP)]
    pick = jnp.where(owner[0] | owner[1], 1.0, 0.0).astype(BF16)
    slot_prob = jnp.sum(
        jnp.where(owner[0], prob_row[0], 0.0) + jnp.where(owner[1], prob_row[1], 0.0),
        axis=1,
        keepdims=True,
    )

    WIDE = 512

    def wide(n):
        return pl.ds(pl.multiple_of(n * WIDE, WIDE), WIDE)

    loads[2].wait()

    CORE_ROWS = SLOTS // NC

    def build_x(t):
        rows = slice(t * CORE_ROWS, (t + 1) * CORE_ROWS)

        def columns(n):
            xs[rows, wide(n)] = dot(pick[rows], tok[:, wide(n)]).astype(BF16)

        loop(0, D // WIDE, columns)

    def build_dy(t):
        rows = slice(t * CORE_ROWS, (t + 1) * CORE_ROWS)

        def columns(n):
            ds[rows, wide(n)] = (dot(pick[rows], og[:, wide(n)]) * slot_prob[rows]).astype(BF16)

        loop(0, D // WIDE, columns)

    build_x(0)
    for load in loads[4:]:
        load.start()
    pl.semaphore_wait(barrier, PEERS - 1 + 2)

    def to_expert(src, dst, send_sem, recv_sem, j, t):
        peer = ahead(x, y, core, t, j)
        return pltpu.make_async_remote_copy(
            src.at[rows_of(t * CHIPS + peer // NC)],
            dst.at[rows_of(j * NC + core)],
            send_sem.at[t * CHIPS + j],
            recv_sem.at[j * NC + core],
            device_id={"expert": peer},
            device_id_type=MESH,
        )

    def own_block(src, dst, recv_sem):
        return pltpu.make_async_copy(
            src.at[rows_of(core * CHIPS + me // NC)], dst.at[rows_of(OWN * NC + core)], recv_sem.at[OWN * NC + core]
        )

    def dispatch(src, dst, send_sem, recv_sem, t):
        loop(0, OWN, lambda j: to_expert(src, dst, send_sem, recv_sem, j, t).start())

        @pl.when(core == t)
        def _():
            own_block(src, dst, recv_sem).start()

        @pl.when(core != t)
        def _():
            to_expert(src, dst, send_sem, recv_sem, OWN, t).start()

    dispatch(xs, xr, xss, xrs, 0)
    loads[3].wait()

    build_dy(0)
    dispatch(ds, dr, dss, drs, 0)
    build_x(1)
    build_dy(1)

    def dispatch_second():
        dispatch(xs, xr, xss, xrs, 1)
        dispatch(ds, dr, dss, drs, 1)

    @pl.when(core == 1)
    def _():
        pl.semaphore_wait(turn, 1)
        dispatch_second()

    def arrived(dst, recv_sem, i):
        pltpu.make_async_copy(dst.at[rows_of(i)], dst.at[rows_of(i)], recv_sem.at[i]).wait()

    TILE = 256
    MX = 256

    def tile(n):
        return pl.ds(pl.multiple_of(n * TILE, TILE), TILE)

    loads[4].wait()
    loads[5].wait()

    def forward(m):
        loop(0, MX // CAP, lambda i: arrived(xr, xrs, m * (MX // CAP) + i))
        rows = pl.ds(pl.multiple_of(m * MX, MX), MX)

        def columns(n):
            g = dot(xr[rows, :], wg[:, tile(n)])
            u = dot(xr[rows, :], wu[:, tile(n)])
            s = 1.0 / (1.0 + jnp.exp(-g))
            gs = g * s
            hid[rows, tile(n)] = (gs * u).astype(BF16)
            cb[rows, tile(n)] = gs
            ca[rows, tile(n)] = u * s * (1.0 + g * (1.0 - s))

        loop(0, H // TILE, columns)

    loop(0, SLOTS // MX, forward)

    loads[6].wait()
    MD = 128

    def backward(m):
        loop(0, MD // CAP, lambda i: arrived(dr, drs, m * (MD // CAP) + i))
        rows = pl.ds(pl.multiple_of(m * MD, MD), MD)

        def columns(n):
            dh = dot(dr[rows, :], wd[:, tile(n)])
            dg[rows, tile(n)] = (dh * ca[rows, tile(n)]).astype(BF16)
            du[rows, tile(n)] = (dh * cb[rows, tile(n)]).astype(BF16)

        loop(0, H // TILE, columns)

    loop(0, SLOTS // MD, backward)

    @pl.when(core == 0)
    def _():
        pl.semaphore_signal(turn, inc=1, device_id={"expert": me + 1}, device_id_type=MESH)

    right_sides = (dg, du, hid)

    def part(shard, half, w, kept):
        cols = pl.ds(pl.multiple_of(shard * SHARD + half * HALF, HALF), HALF)
        if w == 0:
            kept[:] = [jnp.transpose(xr[:, cols])]
        if w == 2:
            kept[:] = [jnp.transpose(dr[:, cols])]
        return dot(kept[0], right_sides[w][...])

    def shard_up(k):
        return lax.rem(z + 4 - (k + 1) // 2 + NZ, NZ), lax.rem(k + 1, 2)

    def shard_down(k):
        return lax.rem(z - 4 + (k + 1) // 2 + NZ, NZ), lax.rem(k, 2)

    def third(w):
        return pl.ds(w * HALF, HALF)

    def pass_on(src, slot, dst, send_sem, recv_sem, k, w, to):
        return pltpu.make_async_remote_copy(
            src.at[slot, third(w)],
            dst.at[k, third(w)],
            send_sem.at[k * 3 + w],
            recv_sem.at[k * 3 + w],
            device_id={"dp": to},
            device_id_type=MESH,
        )

    ways = (
        (shard_up, sp, rp, pss, prs, up),
        (shard_down, sq, rq, qss, qrs, down),
    )

    def first(k):
        kept = [[], []]
        for w in range(3):
            for left, (which, staged, got, send_sem, recv_sem, to) in zip(kept, ways):
                staged[k, third(w)] = part(*which(k), w, left).astype(BF16)
                pass_on(staged, k, got, send_sem, recv_sem, k, w, to).start()

    loop(0, 2, first)

    @pl.when(core == 0)
    def _():
        dispatch_second()

    def to_token(src, dst, send_sem, recv_sem, i):
        j, c = i // NC, lax.rem(i, NC)
        peer = behind(x, y, c, j)
        return pltpu.make_async_remote_copy(
            src.at[rows_of(i)],
            dst.at[rows_of(me)],
            send_sem.at[i],
            recv_sem.at[me],
            device_id={"expert": peer},
            device_id_type=MESH,
        )

    def give_back(src, dst, send_sem, recv_sem, i):
        @pl.when(i == OWN * NC + core)
        def _():
            pltpu.make_async_copy(src.at[rows_of(i)], dst.at[rows_of(me)], recv_sem.at[me]).start()

        @pl.when(i != OWN * NC + core)
        def _():
            to_token(src, dst, send_sem, recv_sem, i).start()

    def outputs(m):
        rows = pl.ds(pl.multiple_of(m * MD, MD), MD)

        def columns(n):
            ov[rows, tile(n)] = dot_rhs_t(hid[rows, :], wd[tile(n), :]).astype(BF16)
            dxv[rows, tile(n)] = (
                dot_rhs_t(dg[rows, :], wg[tile(n), :]) + dot_rhs_t(du[rows, :], wu[tile(n), :])
            ).astype(BF16)

        loop(0, D // TILE, columns)

        def send(i):
            give_back(ov, orv, oss, ors, m * (MD // CAP) + i)
            give_back(dxv, dxr, dxss, dxrs, m * (MD // CAP) + i)

        loop(0, MD // CAP, send)

    def later(k):
        kept = [[], []]
        for w in range(3):
            for left, (which, staged, got, send_sem, recv_sem, to) in zip(kept, ways):
                mine = part(*which(k), w, left)
                pass_on(got, k - 2, got, send_sem, recv_sem, k - 2, w, to).wait_recv()
                got[k - 2, third(w)] = (mine + got[k - 2, third(w)].astype(F32)).astype(BF16)
                pass_on(got, k - 2, got, send_sem, recv_sem, k, w, to).start()

    def outputs_and_later(k):
        outputs(k - 2)
        later(k)

    loop(2, 2 + SLOTS // MD, outputs_and_later)
    loop(2 + SLOTS // MD, PIECES, later)

    loop(0, PEERS, lambda i: arrived(orv, ors, i))
    loop(0, PEERS, lambda i: arrived(dxr, dxrs, i))
    slot_lane = lax.broadcasted_iota(jnp.int32, (TOK, SLOTS), 1).astype(F32)
    route = [slot_lane == slot_col[k] for k in range(TOP)]
    one = [jnp.where(route[k], 1.0, 0.0).astype(BF16) for k in range(TOP)]
    either = jnp.where(route[0] | route[1], 1.0, 0.0).astype(BF16)

    def combine(n):
        mixed[:, wide(n)] = (
            dot(one[0], orv[:, wide(n)]) * prob_col[0] + dot(one[1], orv[:, wide(n)]) * prob_col[1]
        ).astype(BF16)
        tgrad[:, wide(n)] = dot(either, dxr[:, wide(n)]).astype(BF16)

    loop(0, D // WIDE, combine)
    stores = [
        pltpu.make_async_copy(mixed, mixed_hbm, store_sem.at[0]),
        pltpu.make_async_copy(tgrad, tgrad_hbm, store_sem.at[1]),
    ]
    for store in stores:
        store.start()

    for half in range(2):
        left = []
        for w in range(3):
            acc[half, third(w)] = part(z, half, w, left)
    for w, out in enumerate((gg_hbm, gu_hbm, gd_hbm)):
        for k in (PIECES - 2, PIECES - 1):
            pass_on(rp, k, rp, pss, prs, k, w, up).wait_recv()
            pass_on(rq, k, rq, qss, qrs, k, w, down).wait_recv()
        for half, (k_up, k_down) in enumerate(((5, 6), (6, 5))):
            grads[w, half * HALF : (half + 1) * HALF] = (
                acc[half, third(w)] + rp[k_up, third(w)].astype(F32) + rq[k_down, third(w)].astype(F32)
            ).astype(BF16)
        store = pltpu.make_async_copy(grads.at[w], out.at[0], store_sem.at[2 + w])
        store.start()
        stores.append(store)

    def sent(src, dst, send_sem, recv_sem, i):
        to_expert(src, dst, send_sem, recv_sem, lax.rem(i, CHIPS), i // CHIPS).wait_send()

    def all_sent(i):
        @pl.when(i != core * CHIPS + OWN)
        def _():
            sent(xs, xr, xss, xrs, i)
            sent(ds, dr, dss, drs, i)

        @pl.when(i != OWN * NC + core)
        def _():
            to_token(ov, orv, oss, ors, i).wait_send()
            to_token(dxv, dxr, dxss, dxrs, i).wait_send()

    loop(0, PEERS, all_sent)

    def passed(k):
        for w in range(3):
            pass_on(rp, k, rp, pss, prs, k, w, up).wait_send()
            pass_on(rq, k, rq, qss, qrs, k, w, down).wait_send()

    loop(0, PIECES, passed)
    for store in stores:
        store.wait()


def hand_on(*refs):
    count = (len(refs) - 2) // 3
    srcs, dsts, bufs = (refs[i * count : (i + 1) * count] for i in range(3))
    in_sem, out_sem = refs[3 * count :]
    ins = [pltpu.make_async_copy(s, b, in_sem.at[i]) for i, (s, b) in enumerate(zip(srcs, bufs))]
    outs = [pltpu.make_async_copy(b, d, out_sem.at[i]) for i, (b, d) in enumerate(zip(bufs, dsts))]
    for copy in ins:
        copy.start()
    for copy, then in zip(ins, outs):
        copy.wait()
        then.start()
    for copy in outs:
        copy.wait()


def local(tokens, expert_ids, gate_probs, w_gate, w_up, w_down, out_grad):
    hbm = pl.BlockSpec(memory_space=pl.ANY)
    dma = pltpu.SemaphoreType.DMA
    slots = lambda: pltpu.VMEM((SLOTS, D), BF16)
    acts = lambda dtype: pltpu.VMEM((SLOTS, H), dtype)
    shapes = (
        jax.ShapeDtypeStruct((TOK, D), BF16),
        jax.ShapeDtypeStruct((TOK, D), BF16),
        jax.ShapeDtypeStruct((1, SHARD, H), BF16),
        jax.ShapeDtypeStruct((1, SHARD, H), BF16),
        jax.ShapeDtypeStruct((1, SHARD, H), BF16),
    )
    results = pl.pallas_call(
        kernel,
        out_shape=shapes,
        in_specs=[hbm] * 7,
        out_specs=(hbm,) * 5,
        scratch_shapes=[
            pltpu.VMEM((TOP, TOK), jnp.int32),
            pltpu.VMEM((TOP, TOK), F32),
            pltpu.VMEM((TOK, D), BF16),
            pltpu.VMEM((TOK, D), BF16),
            pltpu.VMEM((D, H), BF16),
            pltpu.VMEM((D, H), BF16),
            pltpu.VMEM((D, H), BF16),
            slots(), slots(), slots(), slots(),
            acts(BF16), acts(BF16), acts(BF16), acts(F32), acts(F32),
            slots(), slots(), slots(), slots(),
            pltpu.VMEM((2, 3 * HALF, H), BF16),
            pltpu.VMEM((2, 3 * HALF, H), BF16),
            pltpu.VMEM((PIECES, 3 * HALF, H), BF16),
            pltpu.VMEM((PIECES, 3 * HALF, H), BF16),
            pltpu.VMEM((2, 3 * HALF, H), F32),
            pltpu.VMEM((TOK, D), BF16),
            pltpu.VMEM((TOK, D), BF16),
            pltpu.VMEM((3, SHARD, H), BF16),
            dma((7,)), dma((5,)),
            dma((PEERS,)), dma((PEERS,)), dma((PEERS,)), dma((PEERS,)),
            dma((PEERS,)), dma((PEERS,)), dma((PEERS,)), dma((PEERS,)),
            dma((PIECES * 3,)), dma((PIECES * 3,)), dma((PIECES * 3,)), dma((PIECES * 3,)),
            pltpu.SemaphoreType.REGULAR,
        ],
        compiler_params=pltpu.CompilerParams(
            collective_id=0, has_side_effects=True, vmem_limit_bytes=62 * 2**20
        ),
        name="expert_layer",
    )(expert_ids.T, gate_probs.T, tokens, out_grad, w_gate, w_up, w_down)
    return pl.pallas_call(
        hand_on,
        out_shape=shapes,
        in_specs=[hbm] * 5,
        out_specs=(hbm,) * 5,
        scratch_shapes=[pltpu.VMEM(shape.shape, shape.dtype) for shape in shapes] + [dma((5,)), dma((5,))],
        name="hand_on",
    )(*results)


def solution(mesh):
    placed = (
        P(("dp", "expert"), None),
        P(("dp", "expert"), None),
        P(("dp", "expert"), None),
        P("expert", None, None),
        P("expert", None, None),
        P("expert", None, None),
        P(("dp", "expert"), None),
    )
    return jax.shard_map(
        local,
        mesh=mesh,
        in_specs=placed,
        out_specs=(
            P(("dp", "expert"), None),
            P(("dp", "expert"), None),
            P("expert", "dp", None),
            P("expert", "dp", None),
            P("expert", "dp", None),
        ),
        check_vma=False,
    )
```
